32 devices in a mesh: guide: 2 (over core), seq: 4 (over y, x), fsdp: 4 (over z).
Axes of the slice: x: 2, y: 2, z: 4, core: 2. Of those that a mesh axis runs over, the one named last changes fastest.
Arguments:
- hidden: bfloat16 [2, 1536, 3072], P('guide', 'seq', 'fsdp'), may hold values from -6 to 6
- modulation: float32 [2, 1, 5, 3072], P('guide'), may hold values from -3 to 3
- in_weight: bfloat16 [3072, 21504], P(None, 'fsdp'), may hold values from -0.109375 to 0.109375
- query_gain: float32 [128], replicated, may hold values from 1 to 20
- key_gain: float32 [128], replicated, may hold values from 1 to 20
- out_weight: bfloat16 [15360, 3072], P('fsdp', 'guide'), may hold values from -0.046875 to 0.046875
- head_weight: bfloat16 [3072, 64], replicated, may hold values from -0.109375 to 0.109375
- latents: float32 [64, 1536], P(None, 'seq'), may hold values from -6 to 6
- step_size: float32 [1], replicated, may hold values from -0.6 to -0.15
- guidance: float32 [1], replicated, may hold values from 1.5 to 5
- text_len: int32 [1], replicated, may hold values from 64 to 512, as said below
- tile_map: int32 [12], replicated, may hold values from 0 to 11, each once
Outputs:
- hidden_out: bfloat16 [2, 1536, 3072], P('guide', 'seq', 'fsdp')
- next_latents: float32 [64, 1536], P('guide', 'seq')
- hidden_norm: float32 [2, 1], P('guide')
- head_peak: float32 [2, 1], P('guide')
The draws below stay inside these ranges and needn't reach their ends.
Inputs may be any that keep to these rules, and one draw needn't show every extreme that they name: `text_len`: some request has exactly 512. `tile_map`: each tile number once.
All inputs are finite; a program needn't handle non-finite values.
Results may differ from the reference program's by a relative error of at most 0.01.
Values may be sent and summed in bfloat16 or wider, within the bound.
A program may use at most 192 MiB of HBM per device.

```python
import math
import jax
import jax.numpy as jnp
from jax import lax

D = 3072
HEADS = 24
HD = 128
FF = 12288
CH = 64
TXT = 512
IMG = 1024
TILE = 128
TOKENS = 1536
REQ = 1
NTILES = 12
HG = 6
FFG = 3072
INW = 21504
OUTW = 15360
N_FSDP = 4


def gain_draw(key, salt):
    base = jnp.exp(jax.random.uniform(jax.random.fold_in(key, salt), (HD,), jnp.float32, 0.0, math.log(3.0)))
    return base.astype(jnp.float32)


def draw_query_gain(key, part):
    return gain_draw(key, 21)


def draw_key_gain(key, part):
    return gain_draw(key, 31)


def draw_text_len(key, part):
    counts = jax.random.randint(jax.random.fold_in(key, 1), (REQ,), max(1, TXT // 8), TXT + 1)
    chosen = jax.random.randint(jax.random.fold_in(key, 2), (), 0, REQ)
    return jnp.where(jnp.arange(REQ) == chosen, TXT, counts).astype(jnp.int32)


def block_scale(key, dims, cuts, low, largest):
    def one(axis_at, blocks):
        draws = jax.random.uniform(jax.random.fold_in(jax.random.fold_in(key, 6), axis_at), (blocks,), jnp.float32, low / len(cuts), largest / len(cuts))
        return jnp.repeat(jnp.exp(draws), dims[axis_at] // blocks).reshape((-1,) + (1,) * (len(dims) - axis_at - 1))

    level = one(*cuts[0])
    for cut in cuts[1:]:
        level = level * one(*cut)
    return level


def bell_draw(key, shape, scale, reach, cuts=(), held_as=jnp.bfloat16):
    array = scale * jax.random.normal(key, shape, jnp.float32)
    if cuts:
        array = array * block_scale(key, shape, cuts, -0.22, 0.18)
    return jnp.clip(array, -reach, reach).astype(held_as)


def setup_inputs(seed: int = 0) -> dict:
    splits = jax.random.split(jax.random.key(seed), 13)
    hidden = bell_draw(splits[0], (2, TOKENS, D), 1.0, 6.0, ((0, 2), (1, 4), (2, 4)))
    modulation = bell_draw(splits[1], (2, REQ, 5, D), 0.5, 3.0, ((0, 2),), jnp.float32)
    in_weight = bell_draw(splits[2], (D, INW), D ** -0.5, 0.109375, ((1, 4),))
    query_gain = draw_query_gain(jax.random.fold_in(splits[12], 71), 0)
    key_gain = draw_key_gain(jax.random.fold_in(splits[12], 71), 0)
    out_weight = bell_draw(splits[5], (OUTW, D), OUTW ** -0.5, 0.046875, ((0, 4), (1, 2)))
    head_weight = bell_draw(splits[6], (D, CH), D ** -0.5, 0.109375)
    latents = bell_draw(splits[7], (CH, TOKENS), 1.0, 6.0, ((1, 4),), jnp.float32)
    step_size = jnp.clip(jax.random.uniform(splits[8], (REQ,), jnp.float32, -0.6, -0.15), -0.6, -0.15)
    guidance = jnp.clip(jax.random.uniform(splits[9], (REQ,), jnp.float32, 1.5, 5.0), 1.5, 5.0)
    text_len = draw_text_len(jax.random.fold_in(splits[12], 71), 0)
    tile_map = jax.random.permutation(splits[11], NTILES).astype(jnp.int32)
    return dict(hidden=hidden, modulation=modulation, in_weight=in_weight, query_gain=query_gain, key_gain=key_gain, out_weight=out_weight, head_weight=head_weight, latents=latents, step_size=step_size, guidance=guidance, text_len=text_len, tile_map=tile_map)


def layer_norm(values):
    middle = lax.optimization_barrier(jnp.mean(values, axis=-1, keepdims=True))
    power = lax.optimization_barrier(jnp.mean(values * values, axis=-1, keepdims=True))
    return (values - middle) * lax.rsqrt(power - middle * middle + 1e-06)

def describe(tile_map, text_len):
    index = jnp.arange(TOKENS, dtype=jnp.int32)
    logical = tile_map[index // TILE] * TILE + index % TILE
    request = (logical // (TXT + IMG)).astype(jnp.int32)
    position = logical % (TXT + IMG)
    image = position >= TXT
    valid = image | (position < text_len[request])
    return (request, image, valid)

def head_rms(values, gain):
    scaled = values * lax.rsqrt(lax.optimization_barrier(jnp.mean(values * values, axis=-1, keepdims=True)) + 1e-06)
    return (scaled * gain).astype(jnp.bfloat16)

def one_half(hidden_half, modulation_half, in_weight, query_gain, key_gain, out_weight, head_weight, request, valid):
    keep = valid[:, None]
    x_rows = hidden_half * keep.astype(jnp.bfloat16)
    shift = modulation_half[:, 0, :][request]
    scale = modulation_half[:, 1, :][request]
    gate = modulation_half[:, 2, :][request]
    normed = layer_norm(x_rows.astype(jnp.float32))
    modded = ((1.0 + scale) * normed + shift).astype(jnp.bfloat16)
    projected = jnp.dot(modded, in_weight, preferred_element_type=jnp.float32)
    grouped = projected.reshape(TOKENS, N_FSDP, -1)
    span = HG * HD
    queries = head_rms(grouped[:, :, :span].reshape(TOKENS, HEADS, HD), query_gain)
    keys = head_rms(grouped[:, :, span:2 * span].reshape(TOKENS, HEADS, HD), key_gain)
    values = grouped[:, :, 2 * span:3 * span].reshape(TOKENS, HEADS, HD).astype(jnp.bfloat16)
    mlp_part = grouped[:, :, 3 * span:].reshape(TOKENS, FF)
    allowed = (request[:, None] == request[None, :]) & valid[None, :]
    factor = HD ** (-0.5)

    def attend(operands):
        query_head, key_head, value_head = operands
        scores = jnp.dot(query_head, key_head.T, preferred_element_type=jnp.float32) * factor
        scores = jnp.where(allowed, scores, -jnp.inf)
        top = lax.optimization_barrier(jnp.max(scores, axis=-1, keepdims=True))
        raised = jnp.exp(scores - top)
        total = lax.optimization_barrier(jnp.sum(raised, axis=-1, keepdims=True))
        summed = jnp.dot(raised.astype(jnp.bfloat16), value_head, preferred_element_type=jnp.float32)
        return (summed / total).astype(jnp.bfloat16)
    attended = lax.map(attend, (queries.transpose(1, 0, 2), keys.transpose(1, 0, 2), values.transpose(1, 0, 2)))
    attended = attended.transpose(1, 0, 2).reshape(TOKENS, N_FSDP, span)
    activated = jax.nn.gelu(mlp_part, approximate=True).astype(jnp.bfloat16).reshape(TOKENS, N_FSDP, FFG)
    branch = jnp.concatenate([attended, activated], axis=2).reshape(TOKENS, OUTW)
    mixed = jnp.dot(branch, out_weight, preferred_element_type=jnp.float32)
    updated = ((x_rows.astype(jnp.float32) + gate * mixed) * keep.astype(jnp.float32)).astype(jnp.bfloat16)
    head_shift = modulation_half[:, 3, :][request]
    head_scale = modulation_half[:, 4, :][request]
    final = ((1.0 + head_scale) * layer_norm(updated.astype(jnp.float32)) + head_shift).astype(jnp.bfloat16)
    velocity = jnp.dot(final, head_weight, preferred_element_type=jnp.float32)
    return (updated, velocity)

def reference(hidden, modulation, in_weight, query_gain, key_gain, out_weight, head_weight, latents, step_size, guidance, text_len, tile_map):
    request, image, valid = describe(tile_map, text_len)
    member = request[None, :] == jnp.arange(REQ, dtype=jnp.int32)[:, None]
    updates = []
    velocities = []
    norms = []
    peaks = []
    for half in range(2):
        updated, velocity = one_half(hidden[half], modulation[half], in_weight, query_gain, key_gain, out_weight, head_weight, request, valid)
        squares = lax.optimization_barrier(jnp.sum(jnp.square(updated.astype(jnp.float32)), axis=1))
        total = lax.optimization_barrier(jnp.sum(jnp.where(member & valid[None, :], squares[None, :], 0.0), axis=1))
        count = (IMG + text_len).astype(jnp.float32) * D
        norms.append(jnp.sqrt(total / count))
        picked = jnp.where((member & image[None, :])[:, :, None], velocity[None, :, :], -jnp.inf)
        peaks.append(lax.optimization_barrier(jnp.max(picked, axis=(1, 2))))
        updates.append(updated)
        velocities.append(velocity)
    guided = velocities[1] + guidance[request][:, None] * (velocities[0] - velocities[1])
    stepped = latents.T + step_size[request][:, None] * guided
    next_latents = jnp.where(image[:, None], stepped, 0.0).T
    return (jnp.stack(updates), next_latents, jnp.stack(norms), jnp.stack(peaks))
```

```python
import jax
import jax.numpy as jnp
from jax import lax
from jax.experimental import pallas as pl
from jax.experimental.pallas import tpu as pltpu
from jax.sharding import PartitionSpec as P

HD = 128
TXT = 512
IMG = 1024
TILE = 128


def swapped(block, axis, stride):
    count = lax.axis_size(axis)
    route = []
    for low in range(count):
        high = low | 1 << stride
        if high != low and high < count:
            route += [(low, high), (high, low)]
    return lax.ppermute(block, axis, route)


def layer_norm(values):
    middle = jnp.mean(values, axis=-1, keepdims=True)
    power = jnp.mean(values * values, axis=-1, keepdims=True)
    return (values - middle) * lax.rsqrt(power - middle * middle + 1e-06)


def describe(index, tile_map, text_len):
    tile_index = index // TILE
    numbers = jnp.arange(tile_map.shape[0], dtype=jnp.int32)
    picked = jnp.sum(
        jnp.where(tile_index[:, None] == numbers[None, :], tile_map[None, :], 0), axis=1
    )
    logical = picked * TILE + index % TILE
    request = logical // (TXT + IMG)
    position = logical % (TXT + IMG)
    image = position >= TXT
    slots = jnp.arange(text_len.shape[0], dtype=jnp.int32)
    length = jnp.sum(jnp.where(request[:, None] == slots[None, :], text_len[None, :], 0), axis=1)
    valid = image | (position < length)
    return (request, image, valid)


def head_rms(values, gain):
    row_count = values.shape[0]
    shaped = values.reshape(row_count, -1, HD)
    scaled = shaped * lax.rsqrt(jnp.mean(shaped * shaped, axis=-1, keepdims=True) + 1e-06) * gain
    return scaled.reshape(row_count, -1).astype(jnp.bfloat16)


def shards(
    hidden,
    modulation,
    in_weight,
    query_gain,
    key_gain,
    out_weight,
    head_weight,
    latents,
    step_size,
    guidance,
    text_len,
    tile_map,
):
    row_count = hidden.shape[1]
    local_width = hidden.shape[2]
    requests = text_len.shape[0]
    first_row = lax.axis_index("seq") * row_count
    my_request, my_image, my_valid = describe(
        first_row + jnp.arange(row_count, dtype=jnp.int32), tile_map, text_len
    )
    request_hot = (my_request[:, None] == jnp.arange(requests, dtype=jnp.int32)[None, :]).astype(
        jnp.float32
    )

    def lookup(which):
        return jnp.dot(request_hot, modulation[0, :, which, :], precision=lax.Precision.HIGHEST)

    feature_start = lax.axis_index("fsdp") * local_width
    keep = my_valid[:, None]
    x_rows = hidden[0] * keep.astype(jnp.bfloat16)
    whole = lax.all_gather(x_rows, "fsdp", axis=1, tiled=True)
    normed = layer_norm(whole.astype(jnp.float32))
    modded = ((1.0 + lookup(1)) * normed + lookup(0)).astype(jnp.bfloat16)
    col_width = in_weight.shape[1]
    projected = jnp.dot(modded, in_weight, preferred_element_type=jnp.float32)
    span = (col_width - out_weight.shape[0]) // 2
    head_count = span // HD
    queries = head_rms(projected[:, :span], query_gain)
    keys = head_rms(projected[:, span : 2 * span], key_gain)
    values = projected[:, 2 * span : 3 * span].astype(jnp.bfloat16)
    mlp_part = projected[:, 3 * span :]
    query_heads = queries.reshape(row_count, head_count, HD)
    factor = HD ** (-0.5)
    key_piece = lax.all_gather(keys, "seq", axis=0, tiled=True)
    value_piece = lax.all_gather(values, "seq", axis=0, tiled=True)
    width = key_piece.shape[0]
    key_request, key_image, key_valid = describe(
        jnp.arange(width, dtype=jnp.int32), tile_map, text_len
    )
    allowed = (my_request[:, None] == key_request[None, :]) & key_valid[None, :]
    run_max = jnp.full((head_count, row_count), -1e30, jnp.float32)
    key_heads = key_piece.reshape(width, head_count, HD)
    value_heads = value_piece.reshape(width, head_count, HD)
    scores = (
        jnp.einsum("qhd,khd->hqk", query_heads, key_heads, preferred_element_type=jnp.float32)
        * factor
    )
    scores = jnp.where(allowed[None, :, :], scores, -jnp.inf)
    new_max = jnp.maximum(run_max, jnp.max(scores, axis=-1))
    raised = jnp.exp(scores - new_max[:, :, None])
    new_total = jnp.sum(raised, axis=-1)
    added = jnp.einsum(
        "hqk,khd->hqd", raised.astype(jnp.bfloat16), value_heads, preferred_element_type=jnp.float32
    )
    attended = (
        (added / new_total[:, :, None])
        .transpose(1, 0, 2)
        .reshape(row_count, span)
        .astype(jnp.bfloat16)
    )
    activated = jax.nn.gelu(mlp_part, approximate=True).astype(jnp.bfloat16)
    branch = jnp.concatenate([attended, activated], axis=1)
    terms = jnp.dot(
        branch,
        lax.all_gather(out_weight, "guide", axis=1, tiled=True),
        preferred_element_type=jnp.float32,
    )
    mixed = lax.psum_scatter(terms, "fsdp", scatter_dimension=1, tiled=True)
    gate = lax.dynamic_slice_in_dim(lookup(2), feature_start, local_width, 1)
    updated = ((x_rows.astype(jnp.float32) + gate * mixed) * keep.astype(jnp.float32)).astype(
        jnp.bfloat16
    )
    up_values = updated.astype(jnp.float32)
    contract = (((0,), (1,)), ((), ()))
    full_width = local_width * lax.axis_size("fsdp")
    row_sums, row_squares = lax.psum(
        (jnp.sum(up_values, axis=1), jnp.sum(up_values * up_values, axis=1)), "fsdp"
    )
    middle = (row_sums / full_width)[:, None]
    power = (row_squares / full_width)[:, None]
    local_normed = (up_values - middle) * lax.rsqrt(power - middle * middle + 1e-06)
    head_scale = lax.dynamic_slice_in_dim(lookup(4), feature_start, local_width, 1)
    head_shift = lax.dynamic_slice_in_dim(lookup(3), feature_start, local_width, 1)
    final = ((1.0 + head_scale) * local_normed + head_shift).astype(jnp.bfloat16)
    head_rows = lax.dynamic_slice_in_dim(head_weight, feature_start, local_width, 0)
    head_part = lax.dot_general(head_rows, final, contract, preferred_element_type=jnp.float32)
    velocity = lax.psum(head_part, "fsdp")
    partner = swapped(velocity.astype(jnp.bfloat16), "guide", 0).astype(velocity.dtype)
    is_first = lax.axis_index("guide") == 0
    cond_velocity = jnp.where(is_first, velocity, partner)
    uncond_velocity = jnp.where(is_first, partner, velocity)
    guide_rows = jnp.dot(request_hot, guidance, precision=lax.Precision.HIGHEST)
    step_rows = jnp.dot(request_hot, step_size, precision=lax.Precision.HIGHEST)
    guided = uncond_velocity + guide_rows[None, :] * (cond_velocity - uncond_velocity)
    channel_count = latents.shape[0] // lax.axis_size("guide")
    channel_start = lax.axis_index("guide") * channel_count
    my_guided = lax.dynamic_slice_in_dim(guided, channel_start, channel_count, 0)
    my_latents = lax.dynamic_slice_in_dim(latents, channel_start, channel_count, 0)
    next_latents = jnp.where(my_image[None, :], my_latents + step_rows[None, :] * my_guided, 0.0)
    member = my_request[None, :] == jnp.arange(requests, dtype=jnp.int32)[:, None]
    squares = jnp.sum(up_values * up_values, axis=1)
    local_total = jnp.sum(jnp.where(member & my_valid[None, :], squares[None, :], 0.0), axis=1)
    picked = jnp.where((member & my_image[None, :])[:, None, :], velocity[None, :, :], -jnp.inf)
    local_peak = jnp.max(picked, axis=(1, 2))
    total = lax.psum(local_total, ("seq", "fsdp"))
    peak = lax.pmax(local_peak, "seq")
    count = (IMG + text_len).astype(jnp.float32) * (local_width * lax.axis_size("fsdp"))
    hidden_norm = jnp.sqrt(total / count)
    return (updated[None], next_latents, hidden_norm[None], peak[None])


MESH = pl.DeviceIdType.MESH
BF = jnp.bfloat16
F32 = jnp.float32


def greet(axes):
    barrier = pltpu.get_barrier_semaphore()
    count = 0
    for axis in axes:
        size = lax.axis_size(axis)
        me = lax.axis_index(axis)
        for step in range(1, size):
            pl.semaphore_signal(
                barrier, inc=1, device_id={axis: lax.rem(me + step, size)}, device_id_type=MESH
            )
        count += size - 1
    pl.semaphore_wait(barrier, count)


def push(src, dst, send, recv, axis, target):
    return pltpu.make_async_remote_copy(
        src_ref=src,
        dst_ref=dst,
        send_sem=send,
        recv_sem=recv,
        device_id={axis: target},
        device_id_type=MESH,
    )


def spread(buf, send, recv, axis):
    size = lax.axis_size(axis)
    me = lax.axis_index(axis)
    copies = [
        push(buf.at[me], buf.at[me], send.at[s - 1], recv.at[me], axis, lax.rem(me + s, size))
        for s in range(1, size)
    ]
    for copy in copies:
        copy.start()
    return copies


def collect(buf, send, recv, axis, copies):
    size = lax.axis_size(axis)
    me = lax.axis_index(axis)
    for copy in copies:
        copy.wait_send()
    for s in range(1, size):
        other = lax.rem(me + s, size)
        push(buf.at[other], buf.at[other], send.at[s - 1], recv.at[other], axis, other).wait_recv()


def pack_stats(sums, squares):
    rows = sums.shape[0]
    lane = lax.broadcasted_iota(jnp.int32, (rows, 128), 1)
    both = jnp.where(lane == 0, sums, jnp.where(lane == 1, squares, 0.0))
    return jnp.transpose(both)[:8]


def places(tmap, tlen, first, shape, dim):
    spot = lax.broadcasted_iota(jnp.int32, shape, dim)
    base = jnp.zeros(shape, jnp.int32)
    for j in range(shape[dim] // TILE):
        base = jnp.where(spot >= j * TILE, (tmap[first + j] - j) * TILE, base)
    where = spot + base
    image = where >= TXT
    return image, image | (where < tlen[0])


def row_keep(tmap, tlen, me, rows):
    _, valid = places(tmap, tlen, me * (rows // TILE), (rows, 1), 0)
    return jnp.where(valid, 1.0, 0.0)


def pick(z, values):
    out = values[-1]
    for i in range(len(values) - 2, -1, -1):
        out = jnp.where(z == i, values[i], out)
    return out


CUTS = ((0, 128), (128, 128), (256, 128))
STEP = 128


def key_mask(tmap, tlen, lo, size, rows):
    shape = (1, 4 * size)
    spot = lax.broadcasted_iota(jnp.int32, shape, 1)
    where = jnp.zeros(shape, jnp.int32)
    for src in range(4):
        row = lo
        while row < lo + size:
            here = src * size + row - lo
            tile = (src * rows + row) // TILE
            base = tmap[tile] * TILE + row % TILE - here
            where = jnp.where(spot >= here, spot + base, where)
            row = (row // TILE + 1) * TILE
    return (where >= TXT) | (where < tlen[0])


def layer_kernel(
    tmap, tlen, guide, step, hid, md, qg, kg, head, lats, w, wo,
    up_out, lat_out, norm_out, peak_out, theirs,
    xg, wbuf, mod, q, kb0, kb1, kb2, vb0, vb1, vb2, act, att, high, low, gain,
    sbuf, rbuf, tmp, st, vel, vsend, vrec, line, swap, tot,
    ws, xs, xr, ps, kq, vq, os, gw, ss, rs, ts, tr, us, ur, vs, vr, gs, ks, kr,
):
    z = lax.axis_index("fsdp")
    g = lax.axis_index("guide")
    me = lax.axis_index("seq")
    rows, part = hid.shape
    width = part * 4
    span = q.shape[1]
    tiles = w.shape[1] // span
    steps = rows // STEP
    last = len(CUTS) - 1
    kbuf = (kb0, kb1, kb2)
    vbuf = (vb0, vb1, vb2)
    inner = (z > 0) & (z < 3)
    near_x = me + 1 - 2 * lax.rem(me, 2)
    near_y = lax.rem(me + 2, 4)
    across = 3 - me

    def wcopy(i):
        at = pl.ds(pl.multiple_of(i * span, span), span)
        return pltpu.make_async_copy(w.at[:, at], wbuf.at[:, at], ws.at[i])

    for i in (1, 2, 0, 3, 4, 5, 6):
        wcopy(i).start()
    greet(("fsdp", "seq", "guide"))

    def x_hop(r, c, way, first=False):
        lo, size = CUTS[r]
        target = jnp.minimum(z + 1, 3) if way == 0 else jnp.maximum(z - 1, 0)
        at = pl.ds(lo, size)
        src = hid.at[at, :] if first else xg.at[c, at, :]
        return push(src, xg.at[c, at, :], xs.at[way, r, c], xr.at[r, c], "fsdp", target)

    def x_own(r):
        @pl.when(z < 3)
        def _():
            x_hop(r, z, 0, True).start()

        @pl.when(z > 0)
        def _():
            x_hop(r, z, 1, True).start()

    def x_arrive(r, c):
        x_hop(r, c, 0).wait_recv()

        @pl.when((c < z) & (z < 3))
        def _():
            x_hop(r, c, 0).start()

        @pl.when((c > z) & (z > 0))
        def _():
            x_hop(r, c, 1).start()

    coming = [
        pick(z, [1, 2, 1, 2]),
        pick(z, [2, 0, 3, 1]),
        pick(z, [3, 3, 0, 0]),
    ]
    x_own(0)
    half_rows = wo.shape[0] // 4
    trades = []
    for i in range(4):
        at = pl.ds(i * half_rows, half_rows)
        trades.append(push(wo.at[at, :], theirs.at[at, :], gw.at[0, i], gw.at[1, i], "guide", 1 - g))
    for trade in trades:
        trade.start()
    keep = row_keep(tmap, tlen, me, rows)
    xg[z] = hid[...]

    def key_hop(r, src, at, target):
        size = CUTS[r][1]
        cut = pl.ds(pl.multiple_of(src * size, 16), size)
        return push(
            kbuf[r].at[cut, :], kbuf[r].at[cut, :], ps.at[r, at], kq.at[r, src], "seq", target
        )

    def value_hop(r, src, at, target):
        size = CUTS[r][1]
        cut = pl.ds(pl.multiple_of(src * size, 16), size)
        return push(
            vbuf[r].at[cut, :], vbuf[r].at[cut, :], ps.at[r, at], vq.at[r, src], "seq", target
        )

    def moves(r):
        return [
            key_hop(r, me, 0, near_x),
            value_hop(r, me, 1, near_y),
            key_hop(r, me, 2, near_y),
            value_hop(r, me, 3, near_x),
            key_hop(r, near_x, 4, near_y),
            value_hop(r, near_y, 5, near_x),
        ]

    def kv_relay(r):
        key_hop(r, near_x, 0, near_x).wait_recv()
        moves(r)[4].start()
        value_hop(r, near_y, 1, near_y).wait_recv()
        moves(r)[5].start()

    def kv_rest(r):
        value_hop(r, near_x, 3, near_x).wait_recv()
        key_hop(r, near_y, 2, near_y).wait_recv()
        key_hop(r, across, 4, near_y).wait_recv()
        value_hop(r, across, 5, near_x).wait_recv()

    def out_load(d, low_rows):
        col = pl.ds((d % 2) * part, part)
        if low_rows:
            src = pl.ds(0, span)
            dst = wbuf.at[pl.ds((d // 2) * span, span), pl.ds(4 * part + (d % 2) * part, part)]
            sem = os.at[4 + d]
        else:
            src = pl.ds(span, wbuf.shape[0])
            dst = wbuf.at[:, pl.ds(d * part, part)]
            sem = os.at[d]
        mine = pltpu.make_async_copy(wo.at[src, col], dst, sem)
        other = pltpu.make_async_copy(theirs.at[src, col], dst, sem)
        return mine, other

    def out_start(d, low_rows):
        mine, other = out_load(d, low_rows)

        @pl.when(g == d // 2)
        def _():
            mine.start()

        @pl.when(g != d // 2)
        def _():
            other.start()

    def head_norm(got, gains, dst, to):
        for h in range(span // HD):
            cols = slice(h * HD, (h + 1) * HD)
            vals = got[:, cols]
            scaled = vals * lax.rsqrt(jnp.mean(vals * vals, axis=1, keepdims=True) + 1e-06)
            dst[to, cols] = (scaled * gains[...]).astype(BF)

    def chunk(r):
        lo, size = CUTS[r]
        at = pl.ds(lo, size)
        kept = keep[lo : lo + size]
        sums = jnp.zeros((size, 1), F32)
        squares = jnp.zeros((size, 1), F32)
        for c in range(4):
            vals = xg[c, at, :].astype(F32) * kept
            sums += jnp.sum(vals, axis=1, keepdims=True)
            squares += jnp.sum(vals * vals, axis=1, keepdims=True)
        middle = sums / width
        inv = lax.rsqrt(squares / width - middle * middle + 1e-06)
        for c in range(4):
            cut = slice(c * part, (c + 1) * part)
            vals = xg[c, at, :].astype(F32) * kept
            mod[:size, cut] = (
                (1.0 + md[1:2, cut]) * ((vals - middle) * inv) + md[0:1, cut]
            ).astype(BF)

        def value(i):
            if r == 0:
                wcopy(i).wait()
            at = pl.ds(pl.multiple_of(i * span, span), span)
            return jnp.dot(mod[:size, :], wbuf[:, at], preferred_element_type=F32)

        own = pl.ds(pl.multiple_of(me * size, 16), size)
        head_norm(value(1), kg, kbuf[r], own)
        hops = moves(r)
        hops[0].start()
        vbuf[r][own, :] = value(2).astype(BF)
        for move in hops[1:4]:
            move.start()
        if r < last:
            x_own(r + 1)
        head_norm(value(0), qg, q, at)
        if r == last:
            for trade in trades:
                trade.wait_recv()
            for d in range(3):
                out_start(d, False)

        def tile(i, carry):
            to = pl.ds(pl.multiple_of((i - 3) * span, span), span)
            act[at, to] = jax.nn.gelu(value(i), approximate=True).astype(BF)
            return carry

        lax.fori_loop(3, tiles, tile, 0)
        if r == last:
            out_start(3, False)
            for d in range(4):
                out_start(d, True)

    rate = HD ** (-0.5) * 1.4426950408889634

    def attend(r):
        first = r == 0
        lo, size = CUTS[r]
        open_keys = key_mask(tmap, tlen, lo, size, rows)

        def heads(i, carry):
            for j in range(2):
                h = i * 2 + j
                at = pl.ds(pl.multiple_of(h * HD, HD), HD)
                s = lax.dot_general(
                    q[:, at], kbuf[r][:, at], (((1,), (1,)), ((), ())), preferred_element_type=F32
                )
                s = jnp.where(open_keys, s, -1e30)
                top = jnp.max(s, axis=1, keepdims=True)
                if not first:
                    top = jnp.maximum(top, high[h])
                p = jnp.exp2((s - top) * rate)
                total = jnp.sum(p, axis=1, keepdims=True)
                got = jnp.dot(p.astype(BF), vbuf[r][:, at], preferred_element_type=F32)
                if not first:
                    shrink = jnp.exp2((high[h] - top) * rate)
                    total = total + low[h] * shrink
                    got = got + gain[:, at] * shrink
                if r == last:
                    att[:, at] = (got / total).astype(BF)
                else:
                    high[h] = top
                    low[h] = total
                    gain[:, at] = got
            return carry

        lax.fori_loop(0, span // (2 * HD), heads, 0)

    for r in range(last + 1):
        for c in coming:
            x_arrive(r, c)
        if r > 0:
            kv_relay(r - 1)
        chunk(r)
    kv_rest(0)
    attend(0)
    kv_relay(last)
    kv_rest(1)
    attend(1)
    kv_rest(last)
    attend(last)
    for d in range(4):
        for low_rows in (False, True):
            out_load(d, low_rows)[0].wait()

    def hop(r, p, d, way):
        at = pl.ds(r * STEP, STEP)
        slot = d + 1 - way
        return push(
            sbuf.at[p, at, :], rbuf.at[slot, at, :], ss.at[r, p], rs.at[r, slot], "fsdp",
            jnp.clip(z + 1 - 2 * way, 0, 3),
        )

    def share(d, at):
        col = pl.ds(pl.multiple_of(d * part, part), part)
        up = pl.ds(pl.multiple_of((d // 2) * span, span), span)
        side = pl.ds(pl.multiple_of((4 + d % 2) * part, part), part)
        tmp[...] = jnp.dot(
            act[at, :], wbuf[:, col], preferred_element_type=F32
        ) + jnp.dot(att[at, :], wbuf[up, side], preferred_element_type=F32)

    cut = pl.ds(pl.multiple_of(z * part, part), part)
    weighted = head[:, cut].astype(F32) * (1.0 + md[4:5, cut])
    quarter = vsend.shape[1]

    def order_at(p):
        firsts = pick(z, [3, 3, 0, 0])
        seconds = pick(z, [2, 0, 3, 1])
        thirds = pick(z, [1, 2, 1, 2])
        return jnp.where(p == 0, firsts, jnp.where(p == 1, seconds, thirds))

    for r in range(steps):
        at = pl.ds(r * STEP, STEP)

        def relay(p, carry):
            d = order_at(p)
            way = jnp.where(d > z, 0, 1)
            share(d, at)

            @pl.when(inner)
            def _():
                hop(r, p, d, way).wait_recv()
                tmp[...] += rbuf[d + 1 - way, at, :].astype(F32)

            sbuf[p, at, :] = tmp[...].astype(BF)
            hop(r, p, d, way).start()
            return carry

        lax.fori_loop(0, 3, relay, 0)
        share(z, at)

        @pl.when(z > 0)
        def _():
            hop(r, 0, z, 0).wait_recv()
            tmp[...] += rbuf[z + 1, at, :].astype(F32)

        @pl.when(z < 3)
        def _():
            hop(r, 0, z, 1).wait_recv()
            tmp[...] += rbuf[z, at, :].astype(F32)

        kept = keep[r * STEP : (r + 1) * STEP]
        x = hid[at, :].astype(F32) * kept
        up = ((x + md[2:3, cut] * tmp[...]) * kept).astype(BF)
        up_out[at, :] = up
        wide = up.astype(F32)
        st[z, :, at] = pack_stats(
            jnp.sum(wide, axis=1, keepdims=True), jnp.sum(wide * wide, axis=1, keepdims=True)
        )
        vpart = lax.dot_general(
            weighted,
            wide,
            (((1,), (1,)), ((), ())),
            precision=lax.Precision.HIGHEST,
            preferred_element_type=F32,
        )
        for d in range(4):
            vsend[d, :, at] = vpart[d * quarter : (d + 1) * quarter]

    stats_sent = spread(st, ts, tr, "fsdp")

    def give(d, source, at):
        return push(vsend.at[d], vrec.at[source], us.at[at], ur.at[source], "fsdp", d)

    for s in range(1, 4):
        give(lax.rem(z + s, 4), z, s - 1).start()
    my_image, my_valid = places(tmap, tlen, me * (rows // TILE), (1, rows), 1)
    my_head = head[pl.ds(pl.multiple_of(z * quarter, quarter), quarter), :].astype(F32)
    scale_sum = jnp.sum(my_head * (1.0 + md[4:5, :]), axis=1, keepdims=True)
    shift_sum = jnp.sum(my_head * md[3:4, :], axis=1, keepdims=True)
    collect(st, ts, tr, "fsdp", stats_sent)
    total = st[0] + st[1] + st[2] + st[3]
    middle = total[0:1] / width
    power = total[1:2] / width
    inv = lax.rsqrt(power - middle * middle + 1e-06)
    mine = vsend[z]
    for s in range(1, 4):
        other = lax.rem(z + s, 4)
        give(other, other, s - 1).wait_recv()
        mine = mine + vrec[other]
    vel[z] = inv * (mine - middle * scale_sum) + shift_sum
    sent = spread(vel, vs, vr, "fsdp")
    collect(vel, vs, vr, "fsdp", sent)
    for d in range(4):
        line[d * quarter : (d + 1) * quarter, :] = vel[d]
    velocity = line[...]
    half = lats.shape[0] // 2
    other = 1 - g
    swap[0] = line[pl.ds(pl.multiple_of(other * half, half), half), :]
    cross = push(swap.at[0], swap.at[1], gs.at[0], gs.at[1], "guide", other)
    cross.start()
    full = jnp.sum(jnp.where(my_valid, total[1:2], 0.0), axis=1, keepdims=True)
    top = jnp.max(jnp.where(my_image, velocity, -jnp.inf), axis=1, keepdims=True)
    top = jnp.max(top, axis=0, keepdims=True)
    level = lax.broadcasted_iota(jnp.int32, (8, 128), 0)
    tot[me] = jnp.where(level == 0, full, top)
    sent = spread(tot, ks, kr, "seq")
    collect(tot, ks, kr, "seq", sent)
    added = tot[0] + tot[1] + tot[2] + tot[3]
    peak = jnp.maximum(jnp.maximum(tot[0], tot[1]), jnp.maximum(tot[2], tot[3]))
    count = (IMG + tlen[0]).astype(F32) * width
    norm_out[...] = jnp.sqrt(added[0:1, 0:1] / count)
    peak_out[...] = peak[1:2, 0:1]
    cross.wait()
    own = line[pl.ds(pl.multiple_of(g * half, half), half), :]
    their_half = swap[1]
    cond = jnp.where(g == 0, own, their_half)
    free = jnp.where(g == 0, their_half, own)
    guided = free + guide[0] * (cond - free)
    mine = lats[pl.ds(pl.multiple_of(g * half, half), half), :]
    lat_out[...] = jnp.where(my_image, mine + step[0] * guided, 0.0)
    for r in range(last + 1):
        for move in moves(r):
            move.wait_send()
        for c in range(4):
            @pl.when((z < 3) & (z >= c))
            def _():
                x_hop(r, c, 0).wait_send()

            @pl.when((z > 0) & (z <= c))
            def _():
                x_hop(r, c, 1).wait_send()
    for s in range(1, 4):
        give(lax.rem(z + s, 4), z, s - 1).wait_send()
    for trade in trades:
        trade.wait_send()
    for r in range(steps):
        for p in range(3):
            d = order_at(p)
            hop(r, p, d, jnp.where(d > z, 0, 1)).wait_send()


def vmem(count):
    return [pl.BlockSpec(memory_space=pltpu.VMEM)] * count


def smem(count):
    return [pl.BlockSpec(memory_space=pltpu.SMEM)] * count


def layer(tmap, tlen, guide, step, hid, md, qg, kg, head, lats, w, wo):
    rows, part = hid.shape
    cols = w.shape[1]
    span = (cols - wo.shape[0]) // 2
    wide = cols - 3 * span
    quarter = lats.shape[0] // 4
    chunks = len(CUTS)
    steps = rows // STEP
    dma = pltpu.SemaphoreType.DMA
    shape = jax.ShapeDtypeStruct
    hbm = pl.BlockSpec(memory_space=pltpu.HBM)
    blocks = [pltpu.VMEM((4 * size, span), BF) for _, size in CUTS]
    return pl.pallas_call(
        layer_kernel,
        out_shape=(
            shape((rows, part), BF),
            shape((lats.shape[0] // 2, rows), F32),
            shape((1, 1), F32),
            shape((1, 1), F32),
            shape(wo.shape, BF),
        ),
        in_specs=smem(4) + vmem(6) + [hbm, hbm],
        out_specs=tuple(vmem(4)) + (hbm,),
        scratch_shapes=[
            pltpu.VMEM((4, rows, part), BF),
            pltpu.VMEM(w.shape, BF),
            pltpu.VMEM((max(size for _, size in CUTS), w.shape[0]), BF),
            pltpu.VMEM((rows, span), BF),
        ]
        + blocks
        + blocks
        + [
            pltpu.VMEM((rows, wide), BF),
            pltpu.VMEM((rows, span), BF),
            pltpu.VMEM((span // HD, rows, 1), F32),
            pltpu.VMEM((span // HD, rows, 1), F32),
            pltpu.VMEM((rows, span), F32),
            pltpu.VMEM((3, rows, part), BF),
            pltpu.VMEM((5, rows, part), BF),
            pltpu.VMEM((STEP, part), F32),
            pltpu.VMEM((4, 8, rows), F32),
            pltpu.VMEM((4, quarter, rows), F32),
            pltpu.VMEM((4, quarter, rows), F32),
            pltpu.VMEM((4, quarter, rows), F32),
            pltpu.VMEM(lats.shape, F32),
            pltpu.VMEM((2, lats.shape[0] // 2, rows), F32),
            pltpu.VMEM((4, 8, 128), F32),
            dma((7,)),
            dma((2, chunks, 4)),
            dma((chunks, 4)),
            dma((chunks, 6)),
            dma((chunks, 4)),
            dma((chunks, 4)),
            dma((8,)),
            dma((2, 4)),
            dma((steps, 3)),
            dma((steps, 5)),
            dma((3,)),
            dma((4,)),
            dma((3,)),
            dma((4,)),
            dma((3,)),
            dma((4,)),
            dma((2,)),
            dma((3,)),
            dma((4,)),
        ],
        compiler_params=pltpu.CompilerParams(
            collective_id=1, has_side_effects=True, vmem_limit_bytes=62 << 20
        ),
        cost_estimate=pl.CostEstimate(
            flops=8 * rows * part * cols, bytes_accessed=8 * part * cols, transcendentals=0
        ),
    )(tmap, tlen, guide, step, hid, md, qg, kg, head, lats, w, wo)


def fast_shards(
    hidden,
    modulation,
    in_weight,
    query_gain,
    key_gain,
    out_weight,
    head_weight,
    latents,
    step_size,
    guidance,
    text_len,
    tile_map,
):
    updated, next_latents, norm, peak, _ = layer(
        tile_map, text_len, guidance, step_size, hidden[0], modulation[0, 0], query_gain[None],
        key_gain[None], head_weight.T, latents, in_weight, out_weight,
    )
    return (updated[None], next_latents, norm, peak)


def solution(mesh):
    placed = (
        P("guide", "seq", "fsdp"),
        P("guide", None, None, None),
        P(None, "fsdp"),
        P(),
        P(),
        P("fsdp", "guide"),
        P(),
        P(None, "seq"),
        P(),
        P(),
        P(),
        P(),
    )
    shape = dict(mesh.shape)
    planned = shape["fsdp"] == 4 and shape["seq"] == 4 and shape["guide"] == 2

    def chosen(*args):
        return (fast_shards if planned and args[10].shape[0] == 1 else shards)(*args)

    return jax.shard_map(
        chosen,
        mesh=mesh,
        in_specs=placed,
        out_specs=(
            P("guide", "seq", "fsdp"),
            P("guide", "seq"),
            P("guide", None),
            P("guide", None),
        ),
        check_vma=False,
    )
```

```python
import jax
import jax.numpy as jnp
from jax import lax
from jax.experimental import pallas as pl
from jax.experimental.pallas import tpu as pltpu
from jax.sharding import PartitionSpec as P

HD = 128
TXT = 512
IMG = 1024
TILE = 128


def swapped(block, axis, stride):
    count = lax.axis_size(axis)
    route = []
    for low in range(count):
        high = low | 1 << stride
        if high != low and high < count:
            route += [(low, high), (high, low)]
    return lax.ppermute(block, axis, route)


def layer_norm(values):
    middle = jnp.mean(values, axis=-1, keepdims=True)
    power = jnp.mean(values * values, axis=-1, keepdims=True)
    return (values - middle) * lax.rsqrt(power - middle * middle + 1e-06)


def describe(index, tile_map, text_len):
    tile_index = index // TILE
    numbers = jnp.arange(tile_map.shape[0], dtype=jnp.int32)
    picked = jnp.sum(
        jnp.where(tile_index[:, None] == numbers[None, :], tile_map[None, :], 0), axis=1
    )
    logical = picked * TILE + index % TILE
    request = logical // (TXT + IMG)
    position = logical % (TXT + IMG)
    image = position >= TXT
    slots = jnp.arange(text_len.shape[0], dtype=jnp.int32)
    length = jnp.sum(jnp.where(request[:, None] == slots[None, :], text_len[None, :], 0), axis=1)
    valid = image | (position < length)
    return (request, image, valid)


def head_rms(values, gain):
    row_count = values.shape[0]
    shaped = values.reshape(row_count, -1, HD)
    scaled = shaped * lax.rsqrt(jnp.mean(shaped * shaped, axis=-1, keepdims=True) + 1e-06) * gain
    return scaled.reshape(row_count, -1).astype(jnp.bfloat16)


def shards(
    hidden,
    modulation,
    in_weight,
    query_gain,
    key_gain,
    out_weight,
    head_weight,
    latents,
    step_size,
    guidance,
    text_len,
    tile_map,
):
    row_count = hidden.shape[1]
    local_width = hidden.shape[2]
    requests = text_len.shape[0]
    first_row = lax.axis_index("seq") * row_count
    my_request, my_image, my_valid = describe(
        first_row + jnp.arange(row_count, dtype=jnp.int32), tile_map, text_len
    )
    request_hot = (my_request[:, None] == jnp.arange(requests, dtype=jnp.int32)[None, :]).astype(
        jnp.float32
    )

    def lookup(which):
        return jnp.dot(request_hot, modulation[0, :, which, :], precision=lax.Precision.HIGHEST)

    feature_start = lax.axis_index("fsdp") * local_width
    keep = my_valid[:, None]
    x_rows = hidden[0] * keep.astype(jnp.bfloat16)
    whole = lax.all_gather(x_rows, "fsdp", axis=1, tiled=True)
    normed = layer_norm(whole.astype(jnp.float32))
    modded = ((1.0 + lookup(1)) * normed + lookup(0)).astype(jnp.bfloat16)
    col_width = in_weight.shape[1]
    projected = jnp.dot(modded, in_weight, preferred_element_type=jnp.float32)
    span = (col_width - out_weight.shape[0]) // 2
    head_count = span // HD
    queries = head_rms(projected[:, :span], query_gain)
    keys = head_rms(projected[:, span : 2 * span], key_gain)
    values = projected[:, 2 * span : 3 * span].astype(jnp.bfloat16)
    mlp_part = projected[:, 3 * span :]
    query_heads = queries.reshape(row_count, head_count, HD)
    factor = HD ** (-0.5)
    key_piece = lax.all_gather(keys, "seq", axis=0, tiled=True)
    value_piece = lax.all_gather(values, "seq", axis=0, tiled=True)
    width = key_piece.shape[0]
    key_request, key_image, key_valid = describe(
        jnp.arange(width, dtype=jnp.int32), tile_map, text_len
    )
    allowed = (my_request[:, None] == key_request[None, :]) & key_valid[None, :]
    run_max = jnp.full((head_count, row_count), -1e30, jnp.float32)
    key_heads = key_piece.reshape(width, head_count, HD)
    value_heads = value_piece.reshape(width, head_count, HD)
    scores = (
        jnp.einsum("qhd,khd->hqk", query_heads, key_heads, preferred_element_type=jnp.float32)
        * factor
    )
    scores = jnp.where(allowed[None, :, :], scores, -jnp.inf)
    new_max = jnp.maximum(run_max, jnp.max(scores, axis=-1))
    raised = jnp.exp(scores - new_max[:, :, None])
    new_total = jnp.sum(raised, axis=-1)
    added = jnp.einsum(
        "hqk,khd->hqd", raised.astype(jnp.bfloat16), value_heads, preferred_element_type=jnp.float32
    )
    attended = (
        (added / new_total[:, :, None])
        .transpose(1, 0, 2)
        .reshape(row_count, span)
        .astype(jnp.bfloat16)
    )
    activated = jax.nn.gelu(mlp_part, approximate=True).astype(jnp.bfloat16)
    branch = jnp.concatenate([attended, activated], axis=1)
    terms = jnp.dot(
        branch,
        lax.all_gather(out_weight, "guide", axis=1, tiled=True),
        preferred_element_type=jnp.float32,
    )
    mixed = lax.psum_scatter(terms, "fsdp", scatter_dimension=1, tiled=True)
    gate = lax.dynamic_slice_in_dim(lookup(2), feature_start, local_width, 1)
    updated = ((x_rows.astype(jnp.float32) + gate * mixed) * keep.astype(jnp.float32)).astype(
        jnp.bfloat16
    )
    up_values = updated.astype(jnp.float32)
    contract = (((0,), (1,)), ((), ()))
    full_width = local_width * lax.axis_size("fsdp")
    row_sums, row_squares = lax.psum(
        (jnp.sum(up_values, axis=1), jnp.sum(up_values * up_values, axis=1)), "fsdp"
    )
    middle = (row_sums / full_width)[:, None]
    power = (row_squares / full_width)[:, None]
    local_normed = (up_values - middle) * lax.rsqrt(power - middle * middle + 1e-06)
    head_scale = lax.dynamic_slice_in_dim(lookup(4), feature_start, local_width, 1)
    head_shift = lax.dynamic_slice_in_dim(lookup(3), feature_start, local_width, 1)
    final = ((1.0 + head_scale) * local_normed + head_shift).astype(jnp.bfloat16)
    head_rows = lax.dynamic_slice_in_dim(head_weight, feature_start, local_width, 0)
    head_part = lax.dot_general(head_rows, final, contract, preferred_element_type=jnp.float32)
    velocity = lax.psum(head_part, "fsdp")
    partner = swapped(velocity.astype(jnp.bfloat16), "guide", 0).astype(velocity.dtype)
    is_first = lax.axis_index("guide") == 0
    cond_velocity = jnp.where(is_first, velocity, partner)
    uncond_velocity = jnp.where(is_first, partner, velocity)
    guide_rows = jnp.dot(request_hot, guidance, precision=lax.Precision.HIGHEST)
    step_rows = jnp.dot(request_hot, step_size, precision=lax.Precision.HIGHEST)
    guided = uncond_velocity + guide_rows[None, :] * (cond_velocity - uncond_velocity)
    channel_count = latents.shape[0] // lax.axis_size("guide")
    channel_start = lax.axis_index("guide") * channel_count
    my_guided = lax.dynamic_slice_in_dim(guided, channel_start, channel_count, 0)
    my_latents = lax.dynamic_slice_in_dim(latents, channel_start, channel_count, 0)
    next_latents = jnp.where(my_image[None, :], my_latents + step_rows[None, :] * my_guided, 0.0)
    member = my_request[None, :] == jnp.arange(requests, dtype=jnp.int32)[:, None]
    squares = jnp.sum(up_values * up_values, axis=1)
    local_total = jnp.sum(jnp.where(member & my_valid[None, :], squares[None, :], 0.0), axis=1)
    picked = jnp.where((member & my_image[None, :])[:, None, :], velocity[None, :, :], -jnp.inf)
    local_peak = jnp.max(picked, axis=(1, 2))
    total = lax.psum(local_total, ("seq", "fsdp"))
    peak = lax.pmax(local_peak, "seq")
    count = (IMG + text_len).astype(jnp.float32) * (local_width * lax.axis_size("fsdp"))
    hidden_norm = jnp.sqrt(total / count)
    return (updated[None], next_latents, hidden_norm[None], peak[None])


MESH = pl.DeviceIdType.MESH
BF = jnp.bfloat16
F32 = jnp.float32


def greet():
    barrier = pltpu.get_barrier_semaphore()
    g = lax.axis_index("guide")
    me = lax.axis_index("seq")
    z = lax.axis_index("fsdp")
    for s in range(4):
        for t in range(4):
            if s + t:
                ahead = {"seq": lax.rem(me + s, 4), "fsdp": lax.rem(z + t, 4)}
                pl.semaphore_signal(barrier, inc=1, device_id=ahead, device_id_type=MESH)
    for t in range(4):
        ahead = {"guide": 1 - g, "fsdp": lax.rem(z + t, 4)}
        pl.semaphore_signal(barrier, inc=1, device_id=ahead, device_id_type=MESH)
    pl.semaphore_wait(barrier, 19)


def push_to(src, dst, send, recv, target):
    return pltpu.make_async_remote_copy(
        src_ref=src, dst_ref=dst, send_sem=send, recv_sem=recv, device_id=target, device_id_type=MESH
    )


def push(src, dst, send, recv, axis, target):
    return push_to(src, dst, send, recv, {axis: target})


def pack_stats(sums, squares):
    rows = sums.shape[0]
    lane = lax.broadcasted_iota(jnp.int32, (rows, 128), 1)
    both = jnp.where(lane == 0, sums, jnp.where(lane == 1, squares, 0.0))
    return jnp.transpose(both)[:8]


def places(tmap, tlen, first, shape, dim):
    spot = lax.broadcasted_iota(jnp.int32, shape, dim)
    base = jnp.zeros(shape, jnp.int32)
    for j in range(shape[dim] // TILE):
        base = jnp.where(spot >= j * TILE, (tmap[first + j] - j) * TILE, base)
    where = spot + base
    image = where >= TXT
    return image, image | (where < tlen[...])


def row_keep(tmap, tlen, me, rows):
    _, valid = places(tmap, tlen, me * (rows // TILE), (rows, 1), 0)
    return jnp.where(valid, 1.0, 0.0)


def pick(z, values):
    out = values[-1]
    for i in range(len(values) - 2, -1, -1):
        out = jnp.where(z == i, values[i], out)
    return out


CUTS = ((0, 96), (96, 96), (192, 96), (288, 96))
STEP = 128


def key_mask(tmap, tlen, cuts, rows):
    shape = (1, 4 * sum(size for _, size in cuts))
    spot = lax.broadcasted_iota(jnp.int32, shape, 1)
    where = jnp.zeros(shape, jnp.int32)
    here = 0
    for lo, size in cuts:
        for src in range(4):
            row = lo
            while row < lo + size:
                tile = (src * rows + row) // TILE
                base = tmap[tile] * TILE + row % TILE - here
                where = jnp.where(spot >= here, spot + base, where)
                after = min((row // TILE + 1) * TILE, lo + size)
                here += after - row
                row = after
    return (where >= TXT) | (where < tlen[...])


def layer_kernel(
    tmap, tlen, guide, step, hid, md, qg, kg, head, lats, w, wo,
    up_out, lat_out, norm_out, peak_out, theirs,
    xg, wbuf, mod, q, kbuf, vbuf, act, att, high, low, gain,
    sbuf, rbuf, tmp, vsend, vrec, quart, vel, tot,
    ws, xs, xr, ps, kq, vq, os, gw, ss, rs, us, ur, vs, vr, ks, kr,
):
    z = lax.axis_index("fsdp")
    g = lax.axis_index("guide")
    me = lax.axis_index("seq")
    rows, part = hid.shape
    width = part * 4
    span = q.shape[1]
    tiles = w.shape[1] // span
    steps = rows // STEP
    last = len(CUTS) - 1
    inner = (z > 0) & (z < 3)
    near_x = me + 1 - 2 * lax.rem(me, 2)
    near_y = lax.rem(me + 2, 4)
    across = 3 - me

    def wcopy(i):
        at = pl.ds(pl.multiple_of(i * span, span), span)
        return pltpu.make_async_copy(w.at[:, at], wbuf.at[:, at], ws.at[i])

    for i in (1, 2, 0, 3, 4, 5, 6):
        wcopy(i).start()
    greet()

    def x_hop(r, c, way, first=False):
        lo, size = CUTS[r]
        target = jnp.minimum(z + 1, 3) if way == 0 else jnp.maximum(z - 1, 0)
        at = pl.ds(lo, size)
        src = hid.at[at, :] if first else xg.at[c, at, :]
        return push(src, xg.at[c, at, :], xs.at[way, r, c], xr.at[r, c], "fsdp", target)

    def x_own(r):
        @pl.when(z < 3)
        def _():
            x_hop(r, z, 0, True).start()

        @pl.when(z > 0)
        def _():
            x_hop(r, z, 1, True).start()

    def x_arrive(r, c):
        x_hop(r, c, 0).wait_recv()

        @pl.when((c < z) & (z < 3))
        def _():
            x_hop(r, c, 0).start()

        @pl.when((c > z) & (z > 0))
        def _():
            x_hop(r, c, 1).start()

    coming = [
        pick(z, [1, 2, 1, 2]),
        pick(z, [2, 0, 3, 1]),
        pick(z, [3, 3, 0, 0]),
    ]
    x_own(0)
    half_rows = wo.shape[0] // 4
    trades = []
    for i in range(4):
        at = pl.ds(i * half_rows, half_rows)
        trades.append(push(wo.at[at, :], theirs.at[at, :], gw.at[0, i], gw.at[1, i], "guide", 1 - g))
    for trade in trades:
        trade.start()
    keep = row_keep(tmap, tlen, me, rows)
    xg[z] = hid[...]

    def seat(r, src):
        lo, size = CUTS[r]
        return pl.ds(pl.multiple_of(4 * lo + src * size, 16), size)

    def key_hop(r, src, at, target):
        cut = seat(r, src)
        return push(kbuf.at[cut, :], kbuf.at[cut, :], ps.at[r, at], kq.at[r, src], "seq", target)

    def value_hop(r, src, at, target):
        cut = seat(r, src)
        return push(vbuf.at[cut, :], vbuf.at[cut, :], ps.at[r, at], vq.at[r, src], "seq", target)

    def moves(r):
        return [
            key_hop(r, me, 0, near_x),
            value_hop(r, me, 1, near_y),
            key_hop(r, me, 2, near_y),
            value_hop(r, me, 3, near_x),
            key_hop(r, near_x, 4, near_y),
            value_hop(r, near_y, 5, near_x),
        ]

    def kv_relay(r):
        key_hop(r, near_x, 0, near_x).wait_recv()
        moves(r)[4].start()
        value_hop(r, near_y, 1, near_y).wait_recv()
        moves(r)[5].start()

    def kv_rest(r):
        value_hop(r, near_x, 3, near_x).wait_recv()
        key_hop(r, near_y, 2, near_y).wait_recv()
        key_hop(r, across, 4, near_y).wait_recv()
        value_hop(r, across, 5, near_x).wait_recv()

    def out_load(d, low_rows):
        col = pl.ds((d % 2) * part, part)
        if low_rows:
            src = pl.ds(0, span)
            dst = wbuf.at[pl.ds((d // 2) * span, span), pl.ds(4 * part + (d % 2) * part, part)]
            sem = os.at[4 + d]
        else:
            src = pl.ds(span, wbuf.shape[0])
            dst = wbuf.at[:, pl.ds(d * part, part)]
            sem = os.at[d]
        mine = pltpu.make_async_copy(wo.at[src, col], dst, sem)
        other = pltpu.make_async_copy(theirs.at[src, col], dst, sem)
        return mine, other

    def out_start(d, low_rows):
        mine, other = out_load(d, low_rows)

        @pl.when(g == d // 2)
        def _():
            mine.start()

        @pl.when(g != d // 2)
        def _():
            other.start()

    def head_norm(got, gains, dst, to):
        for h in range(span // HD):
            cols = slice(h * HD, (h + 1) * HD)
            vals = got[:, cols]
            scaled = vals * lax.rsqrt(jnp.mean(vals * vals, axis=1, keepdims=True) + 1e-06)
            dst[to, cols] = (scaled * gains[...]).astype(BF)

    def chunk(r):
        lo, size = CUTS[r]
        at = pl.ds(lo, size)
        kept = keep[lo : lo + size]
        sums = jnp.zeros((size, 1), F32)
        squares = jnp.zeros((size, 1), F32)
        for c in range(4):
            vals = xg[c, at, :].astype(F32) * kept
            sums += jnp.sum(vals, axis=1, keepdims=True)
            squares += jnp.sum(vals * vals, axis=1, keepdims=True)
        middle = sums / width
        inv = lax.rsqrt(squares / width - middle * middle + 1e-06)
        for c in range(4):
            cut = slice(c * part, (c + 1) * part)
            vals = xg[c, at, :].astype(F32) * kept
            mod[:size, cut] = (
                (1.0 + md[1, :, cut]) * ((vals - middle) * inv) + md[0, :, cut]
            ).astype(BF)

        def value(i):
            if r == 0:
                wcopy(i).wait()
            at = pl.ds(pl.multiple_of(i * span, span), span)
            return jnp.dot(mod[:size, :], wbuf[:, at], preferred_element_type=F32)

        own = seat(r, me)
        hops = moves(r)
        head_norm(value(1), kg, kbuf, own)
        hops[0].start()
        vbuf[own, :] = value(2).astype(BF)
        hops[1].start()
        head_norm(value(0), qg, q, at)
        if r == last:
            for trade in trades:
                trade.wait_recv()
            for d in range(3):
                out_start(d, False)

        def tile(i, carry):
            to = pl.ds(pl.multiple_of((i - 3) * span, span), span)
            act[at, to] = jax.nn.gelu(value(i), approximate=True).astype(BF)
            return carry

        if r == last:
            hops[2].start()
            hops[3].start()
        lax.fori_loop(3, tiles, tile, 0)
        if r < last:
            hops[2].start()
            hops[3].start()
        if r == last:
            out_start(3, False)
            for d in range(4):
                out_start(d, True)

    rate = HD ** (-0.5) * 1.4426950408889634

    def attend(begin, end):
        first = begin == 0
        cuts = CUTS[begin:end]
        keys = pl.ds(4 * cuts[0][0], 4 * sum(size for _, size in cuts))
        open_keys = key_mask(tmap, tlen, cuts, rows)

        def heads(i, carry):
            for j in range(2):
                h = i * 2 + j
                at = pl.ds(pl.multiple_of(h * HD, HD), HD)
                s = lax.dot_general(
                    q[:, at], kbuf[keys, at], (((1,), (1,)), ((), ())), preferred_element_type=F32
                )
                s = jnp.where(open_keys, s, -1e30)
                top = jnp.max(s, axis=1, keepdims=True)
                if not first:
                    top = jnp.maximum(top, high[h])
                p = jnp.exp2((s - top) * rate)
                total = jnp.sum(p, axis=1, keepdims=True)
                got = jnp.dot(p.astype(BF), vbuf[keys, at], preferred_element_type=F32)
                if not first:
                    shrink = jnp.exp2((high[h] - top) * rate)
                    total = total + low[h] * shrink
                    got = got + gain[:, at] * shrink
                if end == len(CUTS):
                    att[:, at] = (got / total).astype(BF)
                else:
                    high[h] = top
                    low[h] = total
                    gain[:, at] = got
            return carry

        lax.fori_loop(0, span // (2 * HD), heads, 0)

    def arrive(r):
        for n, c in enumerate(coming):
            x_arrive(r, c)
            if r < last and n < 2:
                @pl.when(inner if n else jnp.logical_not(inner))
                def _():
                    x_own(r + 1)

    arrive(0)
    chunk(0)
    for r in range(1, last + 1):

        @pl.when(inner)
        def _():
            arrive(r)

        kv_relay(r - 1)

        @pl.when(jnp.logical_not(inner))
        def _():
            arrive(r)

        chunk(r)
    kv_relay(last)
    for r in range(last):
        kv_rest(r)
    attend(0, last)
    kv_rest(last)
    attend(last, last + 1)
    for d in range(4):
        for low_rows in (False, True):
            out_load(d, low_rows)[0].wait()

    def hop(r, p, d, way):
        at = pl.ds(r * STEP, STEP)
        slot = d + 1 - way
        return push(
            sbuf.at[p], rbuf.at[slot, at, :], ss.at[p], rs.at[r, slot], "fsdp",
            jnp.clip(z + 1 - 2 * way, 0, 3),
        )

    def share(d, at):
        col = pl.ds(pl.multiple_of(d * part, part), part)
        up = pl.ds(pl.multiple_of((d // 2) * span, span), span)
        side = pl.ds(pl.multiple_of((4 + d % 2) * part, part), part)
        tmp[...] = jnp.dot(
            act[at, :], wbuf[:, col], preferred_element_type=F32
        ) + jnp.dot(att[at, :], wbuf[up, side], preferred_element_type=F32)

    cut = pl.ds(pl.multiple_of(z * part, part), part)
    weighted = head[:, cut].astype(F32) * (1.0 + md[4, :, cut])
    quarter = head.shape[0] // 4
    my_head = head[pl.ds(pl.multiple_of(z * quarter, quarter), quarter), :].astype(F32)
    scale_sum = jnp.sum(my_head * (1.0 + md[4]), axis=1, keepdims=True)
    shift_sum = jnp.sum(my_head * md[3], axis=1, keepdims=True)
    my_image, my_valid = places(tmap, tlen, me * (rows // TILE), (1, rows), 1)
    owner = z // 2

    def order_at(p):
        firsts = pick(z, [3, 3, 0, 0])
        seconds = pick(z, [2, 0, 3, 1])
        thirds = pick(z, [1, 2, 1, 2])
        return jnp.where(p == 0, firsts, jnp.where(p == 1, seconds, thirds))

    def sent_before(r, p):
        d = order_at(p)
        hop(r, p, d, jnp.where(d > z, 0, 1)).wait_send()

    def relays(r):
        at = pl.ds(r * STEP, STEP)

        def relay(p, carry):
            d = order_at(p)
            way = jnp.where(d > z, 0, 1)
            share(d, at)
            if r > 0:
                sent_before(r - 1, p)

            @pl.when(inner)
            def _():
                hop(r, p, d, way).wait_recv()
                tmp[...] += rbuf[d + 1 - way, at, :].astype(F32)

            sbuf[p] = tmp[...].astype(BF)
            hop(r, p, d, way).start()
            return carry

        lax.fori_loop(0, 3, relay, 0)

    def give(r, d, source, at):
        return push(vsend.at[r, d], vrec.at[r, source], us.at[r, at], ur.at[r, source], "fsdp", d)

    def final(r):
        at = pl.ds(r * STEP, STEP)
        share(z, at)

        @pl.when(z > 0)
        def _():
            hop(r, 0, z, 0).wait_recv()
            tmp[...] += rbuf[z + 1, at, :].astype(F32)

        @pl.when(z < 3)
        def _():
            hop(r, 0, z, 1).wait_recv()
            tmp[...] += rbuf[z, at, :].astype(F32)

        kept = keep[r * STEP : (r + 1) * STEP]
        x = hid[at, :].astype(F32) * kept
        up = ((x + md[2, :, cut] * tmp[...]) * kept).astype(BF)
        up_out[at, :] = up
        wide = up.astype(F32)
        stats = pack_stats(
            jnp.sum(wide, axis=1, keepdims=True), jnp.sum(wide * wide, axis=1, keepdims=True)
        )
        vpart = lax.dot_general(
            weighted,
            wide,
            (((1,), (1,)), ((), ())),
            precision=lax.Precision.HIGHEST,
            preferred_element_type=F32,
        )
        for d in range(4):
            vsend[r, d, :quarter, :] = vpart[d * quarter : (d + 1) * quarter]
            vsend[r, d, quarter:, :] = stats
        for s in range(1, 4):
            give(r, lax.rem(z + s, 4), z, s - 1).start()

    def vel_move(r, t, source_g, source_z):
        slot = source_g * 2 + lax.rem(source_z, 2)
        return push_to(
            quart.at[r], vel.at[r, slot], vs.at[r, t], vr.at[r, slot],
            {"guide": source_z // 2, "fsdp": lax.rem(z + t, 4)},
        )

    def velocity(r):
        got = vsend[r, z]
        for s in range(1, 4):
            other = lax.rem(z + s, 4)
            give(r, other, other, s - 1).wait_recv()
            got = got + vrec[r, other]
        sums = got[quarter : quarter + 1]
        squares = got[quarter + 1 : quarter + 2]
        middle = sums / width
        inv = lax.rsqrt(squares / width - middle * middle + 1e-06)
        found = inv * (got[:quarter] - middle * scale_sum) + shift_sum
        quart[r] = found
        for t in range(1, 4):
            vel_move(r, t, g, z).start()

        @pl.when(owner != g)
        def _():
            vel_move(r, 0, g, z).start()

        @pl.when(owner == g)
        def _():
            vel[r, g * 2 + lax.rem(z, 2)] = found

        on = slice(r * STEP, (r + 1) * STEP)
        full = jnp.sum(jnp.where(my_valid[:, on], squares, 0.0), axis=1, keepdims=True)
        top = jnp.max(jnp.where(my_image[:, on], found, -jnp.inf), axis=1, keepdims=True)
        return full, jnp.max(top, axis=0, keepdims=True)

    relays(0)
    relays(1)
    final(0)
    relays(2)
    final(1)
    full, top = velocity(0)
    final(2)
    for r in (1, 2):
        more, higher = velocity(r)
        full = full + more
        top = jnp.maximum(top, higher)
    level = lax.broadcasted_iota(jnp.int32, (8, 128), 0)
    tot[z, me] = jnp.where(level == 0, full, top)

    def announce(s, t):
        return push_to(
            tot.at[z, me], tot.at[z, me], ks.at[s, t], kr.at[z, me],
            {"seq": lax.rem(me + s, 4), "fsdp": lax.rem(z + t, 4)},
        )

    pairs = [(s, t) for s in range(4) for t in range(4) if s + t]
    for s, t in pairs:
        announce(s, t).start()
    half = lats.shape[0] // 2
    for r in range(steps):
        for source_g in range(2):
            for turn in range(2):
                slot = source_g * 2 + turn

                @pl.when((g != source_g) | (z != g * 2 + turn))
                def _():
                    push_to(
                        quart.at[r], vel.at[r, slot], vs.at[r, 0], vr.at[r, slot], {"guide": 1 - g}
                    ).wait_recv()

        cond = jnp.concatenate([vel[r, 0], vel[r, 1]], axis=0)
        free = jnp.concatenate([vel[r, 2], vel[r, 3]], axis=0)
        guided = free + guide[...] * (cond - free)
        at = pl.ds(r * STEP, STEP)
        mine = lats[pl.ds(pl.multiple_of(g * half, half), half), at]
        on = slice(r * STEP, (r + 1) * STEP)
        lat_out[:, at] = jnp.where(my_image[:, on], mine + step[...] * guided, 0.0)
    for s, t in pairs:
        there = (lax.rem(z + t, 4), lax.rem(me + s, 4))
        push_to(tot.at[there], tot.at[there], ks.at[s, t], kr.at[there], {"guide": 1 - g}).wait_recv()
    added = tot[z, 0] + tot[z, 1] + tot[z, 2] + tot[z, 3]
    peak = tot[0, 0]
    for s in range(4):
        for t in range(4):
            peak = jnp.maximum(peak, tot[t, s])
    count = (IMG + tlen[...]).astype(F32) * width
    norm_out[...] = jnp.sqrt(added[0:1, 0:1] / count)
    peak_out[...] = peak[1:2, 0:1]
    for r in range(last + 1):
        for move in moves(r):
            move.wait_send()
        for c in range(4):
            @pl.when((z < 3) & (z >= c))
            def _():
                x_hop(r, c, 0).wait_send()

            @pl.when((z > 0) & (z <= c))
            def _():
                x_hop(r, c, 1).wait_send()
    for trade in trades:
        trade.wait_send()
    for p in range(3):
        sent_before(steps - 1, p)
    for r in range(steps):
        for t in range(1, 4):
            give(r, lax.rem(z + t, 4), z, t - 1).wait_send()
            vel_move(r, t, g, z).wait_send()

        @pl.when(owner != g)
        def _():
            vel_move(r, 0, g, z).wait_send()
    for s, t in pairs:
        announce(s, t).wait_send()


def hand_over(up, lat, norm, peak, up_out, lat_out, norm_out, peak_out):
    up_out[...] = up[...]
    lat_out[...] = lat[...]
    norm_out[...] = norm[...]
    peak_out[...] = peak[...]


def vmem(count):
    return [pl.BlockSpec(memory_space=pltpu.VMEM)] * count


def smem(count):
    return [pl.BlockSpec(memory_space=pltpu.SMEM)] * count


def layer(tmap, tlen, guide, step, hid, md, qg, kg, head, lats, w, wo):
    rows, part = hid.shape
    cols = w.shape[1]
    span = (cols - wo.shape[0]) // 2
    wide = cols - 3 * span
    quarter = lats.shape[0] // 4
    chunks = len(CUTS)
    steps = rows // STEP
    dma = pltpu.SemaphoreType.DMA
    shape = jax.ShapeDtypeStruct
    hbm = pl.BlockSpec(memory_space=pltpu.HBM)
    return pl.pallas_call(
        layer_kernel,
        out_shape=(
            shape((rows, part), BF),
            shape((lats.shape[0] // 2, rows), F32),
            shape((1, 1), F32),
            shape((1, 1), F32),
            shape(wo.shape, BF),
        ),
        in_specs=smem(1) + vmem(9) + [hbm, hbm],
        out_specs=tuple(vmem(4)) + (hbm,),
        scratch_shapes=[
            pltpu.VMEM((4, rows, part), BF),
            pltpu.VMEM(w.shape, BF),
            pltpu.VMEM((max(size for _, size in CUTS), w.shape[0]), BF),
            pltpu.VMEM((rows, span), BF),
        ]
        + [
            pltpu.VMEM((4 * rows, span), BF),
            pltpu.VMEM((4 * rows, span), BF),
            pltpu.VMEM((rows, wide), BF),
            pltpu.VMEM((rows, span), BF),
            pltpu.VMEM((span // HD, rows, 1), F32),
            pltpu.VMEM((span // HD, rows, 1), F32),
            pltpu.VMEM((rows, span), F32),
            pltpu.VMEM((3, STEP, part), BF),
            pltpu.VMEM((5, rows, part), BF),
            pltpu.VMEM((STEP, part), F32),
            pltpu.VMEM((steps, 4, quarter + 8, STEP), F32),
            pltpu.VMEM((steps, 4, quarter + 8, STEP), F32),
            pltpu.VMEM((steps, quarter, STEP), F32),
            pltpu.VMEM((steps, 4, quarter, STEP), F32),
            pltpu.VMEM((4, 4, 8, 128), F32),
            dma((7,)),
            dma((2, chunks, 4)),
            dma((chunks, 4)),
            dma((chunks, 6)),
            dma((chunks, 4)),
            dma((chunks, 4)),
            dma((8,)),
            dma((2, 4)),
            dma((3,)),
            dma((steps, 5)),
            dma((steps, 3)),
            dma((steps, 4)),
            dma((steps, 4)),
            dma((steps, 4)),
            dma((4, 4)),
            dma((4, 4)),
        ],
        compiler_params=pltpu.CompilerParams(
            collective_id=1, has_side_effects=True, vmem_limit_bytes=62 << 20
        ),
        cost_estimate=pl.CostEstimate(
            flops=8 * rows * part * cols, bytes_accessed=8 * part * cols, transcendentals=0
        ),
    )(tmap, tlen, guide, step, hid, md, qg, kg, head, lats, w, wo)


def fast_shards(
    hidden,
    modulation,
    in_weight,
    query_gain,
    key_gain,
    out_weight,
    head_weight,
    latents,
    step_size,
    guidance,
    text_len,
    tile_map,
):
    results = layer(
        tile_map, text_len[None], guidance[None], step_size[None], hidden[0],
        modulation[0, 0][:, None, :], query_gain[None], key_gain[None], head_weight.T, latents,
        in_weight, out_weight,
    )[:4]
    updated, next_latents, norm, peak = pl.pallas_call(
        hand_over,
        out_shape=tuple(jax.ShapeDtypeStruct(x.shape, x.dtype) for x in results),
        in_specs=vmem(4),
        out_specs=tuple(vmem(4)),
    )(*results)
    return (updated[None], next_latents, norm, peak)


def solution(mesh):
    placed = (
        P("guide", "seq", "fsdp"),
        P("guide", None, None, None),
        P(None, "fsdp"),
        P(),
        P(),
        P("fsdp", "guide"),
        P(),
        P(None, "seq"),
        P(),
        P(),
        P(),
        P(),
    )
    shape = dict(mesh.shape)
    planned = shape["fsdp"] == 4 and shape["seq"] == 4 and shape["guide"] == 2

    def chosen(*args):
        return (fast_shards if planned and args[10].shape[0] == 1 else shards)(*args)

    return jax.shard_map(
        chosen,
        mesh=mesh,
        in_specs=placed,
        out_specs=(
            P("guide", "seq", "fsdp"),
            P("guide", "seq"),
            P("guide", None),
            P("guide", None),
        ),
        check_vma=False,
    )
```

```python
import jax
import jax.numpy as jnp
from jax import lax
from jax.experimental import pallas as pl
from jax.experimental.pallas import tpu as pltpu
from jax.sharding import PartitionSpec as P

HD = 128
TXT = 512
IMG = 1024
TILE = 128


def swapped(block, axis, stride):
    count = lax.axis_size(axis)
    route = []
    for low in range(count):
        high = low | 1 << stride
        if high != low and high < count:
            route += [(low, high), (high, low)]
    return lax.ppermute(block, axis, route)


def layer_norm(values):
    middle = jnp.mean(values, axis=-1, keepdims=True)
    power = jnp.mean(values * values, axis=-1, keepdims=True)
    return (values - middle) * lax.rsqrt(power - middle * middle + 1e-06)


def describe(index, tile_map, text_len):
    tile_index = index // TILE
    numbers = jnp.arange(tile_map.shape[0], dtype=jnp.int32)
    picked = jnp.sum(
        jnp.where(tile_index[:, None] == numbers[None, :], tile_map[None, :], 0), axis=1
    )
    logical = picked * TILE + index % TILE
    request = logical // (TXT + IMG)
    position = logical % (TXT + IMG)
    image = position >= TXT
    slots = jnp.arange(text_len.shape[0], dtype=jnp.int32)
    length = jnp.sum(jnp.where(request[:, None] == slots[None, :], text_len[None, :], 0), axis=1)
    valid = image | (position < length)
    return (request, image, valid)


def head_rms(values, gain):
    row_count = values.shape[0]
    shaped = values.reshape(row_count, -1, HD)
    scaled = shaped * lax.rsqrt(jnp.mean(shaped * shaped, axis=-1, keepdims=True) + 1e-06) * gain
    return scaled.reshape(row_count, -1).astype(jnp.bfloat16)


def shards(
    hidden,
    modulation,
    in_weight,
    query_gain,
    key_gain,
    out_weight,
    head_weight,
    latents,
    step_size,
    guidance,
    text_len,
    tile_map,
):
    row_count = hidden.shape[1]
    local_width = hidden.shape[2]
    requests = text_len.shape[0]
    first_row = lax.axis_index("seq") * row_count
    my_request, my_image, my_valid = describe(
        first_row + jnp.arange(row_count, dtype=jnp.int32), tile_map, text_len
    )
    request_hot = (my_request[:, None] == jnp.arange(requests, dtype=jnp.int32)[None, :]).astype(
        jnp.float32
    )

    def lookup(which):
        return jnp.dot(request_hot, modulation[0, :, which, :], precision=lax.Precision.HIGHEST)

    feature_start = lax.axis_index("fsdp") * local_width
    keep = my_valid[:, None]
    x_rows = hidden[0] * keep.astype(jnp.bfloat16)
    whole = lax.all_gather(x_rows, "fsdp", axis=1, tiled=True)
    normed = layer_norm(whole.astype(jnp.float32))
    modded = ((1.0 + lookup(1)) * normed + lookup(0)).astype(jnp.bfloat16)
    col_width = in_weight.shape[1]
    projected = jnp.dot(modded, in_weight, preferred_element_type=jnp.float32)
    span = (col_width - out_weight.shape[0]) // 2
    head_count = span // HD
    queries = head_rms(projected[:, :span], query_gain)
    keys = head_rms(projected[:, span : 2 * span], key_gain)
    values = projected[:, 2 * span : 3 * span].astype(jnp.bfloat16)
    mlp_part = projected[:, 3 * span :]
    query_heads = queries.reshape(row_count, head_count, HD)
    factor = HD ** (-0.5)
    key_piece = lax.all_gather(keys, "seq", axis=0, tiled=True)
    value_piece = lax.all_gather(values, "seq", axis=0, tiled=True)
    width = key_piece.shape[0]
    key_request, key_image, key_valid = describe(
        jnp.arange(width, dtype=jnp.int32), tile_map, text_len
    )
    allowed = (my_request[:, None] == key_request[None, :]) & key_valid[None, :]
    run_max = jnp.full((head_count, row_count), -1e30, jnp.float32)
    key_heads = key_piece.reshape(width, head_count, HD)
    value_heads = value_piece.reshape(width, head_count, HD)
    scores = (
        jnp.einsum("qhd,khd->hqk", query_heads, key_heads, preferred_element_type=jnp.float32)
        * factor
    )
    scores = jnp.where(allowed[None, :, :], scores, -jnp.inf)
    new_max = jnp.maximum(run_max, jnp.max(scores, axis=-1))
    raised = jnp.exp(scores - new_max[:, :, None])
    new_total = jnp.sum(raised, axis=-1)
    added = jnp.einsum(
        "hqk,khd->hqd", raised.astype(jnp.bfloat16), value_heads, preferred_element_type=jnp.float32
    )
    attended = (
        (added / new_total[:, :, None])
        .transpose(1, 0, 2)
        .reshape(row_count, span)
        .astype(jnp.bfloat16)
    )
    activated = jax.nn.gelu(mlp_part, approximate=True).astype(jnp.bfloat16)
    branch = jnp.concatenate([attended, activated], axis=1)
    terms = jnp.dot(
        branch,
        lax.all_gather(out_weight, "guide", axis=1, tiled=True),
        preferred_element_type=jnp.float32,
    )
    mixed = lax.psum_scatter(terms, "fsdp", scatter_dimension=1, tiled=True)
    gate = lax.dynamic_slice_in_dim(lookup(2), feature_start, local_width, 1)
    updated = ((x_rows.astype(jnp.float32) + gate * mixed) * keep.astype(jnp.float32)).astype(
        jnp.bfloat16
    )
    up_values = updated.astype(jnp.float32)
    contract = (((0,), (1,)), ((), ()))
    full_width = local_width * lax.axis_size("fsdp")
    row_sums, row_squares = lax.psum(
        (jnp.sum(up_values, axis=1), jnp.sum(up_values * up_values, axis=1)), "fsdp"
    )
    middle = (row_sums / full_width)[:, None]
    power = (row_squares / full_width)[:, None]
    local_normed = (up_values - middle) * lax.rsqrt(power - middle * middle + 1e-06)
    head_scale = lax.dynamic_slice_in_dim(lookup(4), feature_start, local_width, 1)
    head_shift = lax.dynamic_slice_in_dim(lookup(3), feature_start, local_width, 1)
    final = ((1.0 + head_scale) * local_normed + head_shift).astype(jnp.bfloat16)
    head_rows = lax.dynamic_slice_in_dim(head_weight, feature_start, local_width, 0)
    head_part = lax.dot_general(head_rows, final, contract, preferred_element_type=jnp.float32)
    velocity = lax.psum(head_part, "fsdp")
    partner = swapped(velocity.astype(jnp.bfloat16), "guide", 0).astype(velocity.dtype)
    is_first = lax.axis_index("guide") == 0
    cond_velocity = jnp.where(is_first, velocity, partner)
    uncond_velocity = jnp.where(is_first, partner, velocity)
    guide_rows = jnp.dot(request_hot, guidance, precision=lax.Precision.HIGHEST)
    step_rows = jnp.dot(request_hot, step_size, precision=lax.Precision.HIGHEST)
    guided = uncond_velocity + guide_rows[None, :] * (cond_velocity - uncond_velocity)
    channel_count = latents.shape[0] // lax.axis_size("guide")
    channel_start = lax.axis_index("guide") * channel_count
    my_guided = lax.dynamic_slice_in_dim(guided, channel_start, channel_count, 0)
    my_latents = lax.dynamic_slice_in_dim(latents, channel_start, channel_count, 0)
    next_latents = jnp.where(my_image[None, :], my_latents + step_rows[None, :] * my_guided, 0.0)
    member = my_request[None, :] == jnp.arange(requests, dtype=jnp.int32)[:, None]
    squares = jnp.sum(up_values * up_values, axis=1)
    local_total = jnp.sum(jnp.where(member & my_valid[None, :], squares[None, :], 0.0), axis=1)
    picked = jnp.where((member & my_image[None, :])[:, None, :], velocity[None, :, :], -jnp.inf)
    local_peak = jnp.max(picked, axis=(1, 2))
    total = lax.psum(local_total, ("seq", "fsdp"))
    peak = lax.pmax(local_peak, "seq")
    count = (IMG + text_len).astype(jnp.float32) * (local_width * lax.axis_size("fsdp"))
    hidden_norm = jnp.sqrt(total / count)
    return (updated[None], next_latents, hidden_norm[None], peak[None])


MESH = pl.DeviceIdType.MESH
BF = jnp.bfloat16
F32 = jnp.float32


def greet():
    barrier = pltpu.get_barrier_semaphore()
    g = lax.axis_index("guide")
    me = lax.axis_index("seq")
    z = lax.axis_index("fsdp")
    for s in range(4):
        for t in range(4):
            if s + t:
                ahead = {"seq": lax.rem(me + s, 4), "fsdp": lax.rem(z + t, 4)}
                pl.semaphore_signal(barrier, inc=1, device_id=ahead, device_id_type=MESH)
    for t in range(4):
        ahead = {"guide": 1 - g, "fsdp": lax.rem(z + t, 4)}
        pl.semaphore_signal(barrier, inc=1, device_id=ahead, device_id_type=MESH)
    pl.semaphore_wait(barrier, 19)


def push_to(src, dst, send, recv, target):
    return pltpu.make_async_remote_copy(
        src_ref=src, dst_ref=dst, send_sem=send, recv_sem=recv, device_id=target, device_id_type=MESH
    )


def push(src, dst, send, recv, axis, target):
    return push_to(src, dst, send, recv, {axis: target})


def pack_stats(sums, squares):
    rows = sums.shape[0]
    lane = lax.broadcasted_iota(jnp.int32, (rows, 128), 1)
    both = jnp.where(lane == 0, sums, jnp.where(lane == 1, squares, 0.0))
    return jnp.transpose(both)[:8]


def places(tmap, tlen, first, shape, dim):
    spot = lax.broadcasted_iota(jnp.int32, shape, dim)
    base = jnp.zeros(shape, jnp.int32)
    for j in range(shape[dim] // TILE):
        base = jnp.where(spot >= j * TILE, (tmap[first + j] - j) * TILE, base)
    where = spot + base
    image = where >= TXT
    return image, image | (where < tlen[...])


def row_keep(tmap, tlen, me, rows):
    _, valid = places(tmap, tlen, me * (rows // TILE), (rows, 1), 0)
    return jnp.where(valid, 1.0, 0.0)


def pick(z, values):
    out = values[-1]
    for i in range(len(values) - 2, -1, -1):
        out = jnp.where(z == i, values[i], out)
    return out


CUTS = ((0, 96), (96, 96), (192, 96), (288, 96))
STEP = 128


def key_mask(tmap, tlen, cuts, rows):
    shape = (1, 4 * sum(size for _, size in cuts))
    spot = lax.broadcasted_iota(jnp.int32, shape, 1)
    where = jnp.zeros(shape, jnp.int32)
    here = 0
    for lo, size in cuts:
        for src in range(4):
            row = lo
            while row < lo + size:
                tile = (src * rows + row) // TILE
                base = tmap[tile] * TILE + row % TILE - here
                where = jnp.where(spot >= here, spot + base, where)
                after = min((row // TILE + 1) * TILE, lo + size)
                here += after - row
                row = after
    return jnp.where((where >= TXT) | (where < tlen[...]), 0.0, -1e30)


def layer_kernel(
    tmap, tlen, guide, step, hid, md, qg, kg, head, lats, w, wo,
    up_out, lat_out, norm_out, peak_out, theirs,
    xg, wbuf, mod, q, kbuf, vbuf, act, att, high, low, gain,
    sbuf, rbuf, tmp, vsend, vrec, quart, vel, tot, shut, upbuf,
    ws, xs, xr, ps, kq, vq, os, gw, ss, rs, us, ur, vs, vr, ks, kr, uo,
):
    z = lax.axis_index("fsdp")
    g = lax.axis_index("guide")
    me = lax.axis_index("seq")
    rows, part = hid.shape
    width = part * 4
    span = q.shape[1]
    tiles = w.shape[1] // span
    steps = rows // STEP
    last = len(CUTS) - 1
    inner = (z > 0) & (z < 3)
    near_x = me + 1 - 2 * lax.rem(me, 2)
    near_y = lax.rem(me + 2, 4)
    across = 3 - me

    def wcopy(i):
        at = pl.ds(pl.multiple_of(i * span, span), span)
        return pltpu.make_async_copy(w.at[:, at], wbuf.at[:, at], ws.at[i])

    for i in (1, 2, 0, 3, 4, 5, 6):
        wcopy(i).start()
    greet()

    def x_hop(r, c, way, first=False):
        lo, size = CUTS[r]
        target = jnp.minimum(z + 1, 3) if way == 0 else jnp.maximum(z - 1, 0)
        at = pl.ds(lo, size)
        src = hid.at[at, :] if first else xg.at[c, at, :]
        return push(src, xg.at[c, at, :], xs.at[way, r, c], xr.at[r, c], "fsdp", target)

    def x_own(r):
        @pl.when(z < 3)
        def _():
            x_hop(r, z, 0, True).start()

        @pl.when(z > 0)
        def _():
            x_hop(r, z, 1, True).start()

    def x_arrive(r, c):
        x_hop(r, c, 0).wait_recv()

        @pl.when((c < z) & (z < 3))
        def _():
            x_hop(r, c, 0).start()

        @pl.when((c > z) & (z > 0))
        def _():
            x_hop(r, c, 1).start()

    coming = [
        pick(z, [1, 2, 1, 2]),
        pick(z, [2, 0, 3, 1]),
        pick(z, [3, 3, 0, 0]),
    ]
    x_own(0)

    @pl.when(jnp.logical_not(inner))
    def _():
        x_own(1)

    half_rows = wo.shape[0] // 4
    trades = []
    for i in range(4):
        at = pl.ds(i * half_rows, half_rows)
        trades.append(push(wo.at[at, :], theirs.at[at, :], gw.at[0, i], gw.at[1, i], "guide", 1 - g))
    for trade in trades:
        trade.start()
    keep = row_keep(tmap, tlen, me, rows)
    xg[z] = hid[...]

    def seat(r, src):
        lo, size = CUTS[r]
        return pl.ds(pl.multiple_of(4 * lo + src * size, 16), size)

    def key_hop(r, src, at, target):
        cut = seat(r, src)
        return push(kbuf.at[cut, :], kbuf.at[cut, :], ps.at[r, at], kq.at[r, src], "seq", target)

    def value_hop(r, src, at, target):
        cut = seat(r, src)
        return push(vbuf.at[cut, :], vbuf.at[cut, :], ps.at[r, at], vq.at[r, src], "seq", target)

    def moves(r):
        return [
            key_hop(r, me, 0, near_x),
            value_hop(r, me, 1, near_y),
            key_hop(r, me, 2, near_y),
            value_hop(r, me, 3, near_x),
            key_hop(r, near_x, 4, near_y),
            value_hop(r, near_y, 5, near_x),
        ]

    def kv_relay(r):
        key_hop(r, near_x, 0, near_x).wait_recv()
        moves(r)[4].start()
        value_hop(r, near_y, 1, near_y).wait_recv()
        moves(r)[5].start()

    def kv_rest(r):
        value_hop(r, near_x, 3, near_x).wait_recv()
        key_hop(r, near_y, 2, near_y).wait_recv()
        key_hop(r, across, 4, near_y).wait_recv()
        value_hop(r, across, 5, near_x).wait_recv()

    def out_load(d, low_rows):
        col = pl.ds((d % 2) * part, part)
        if low_rows:
            src = pl.ds(0, span)
            dst = wbuf.at[pl.ds((d // 2) * span, span), pl.ds(4 * part + (d % 2) * part, part)]
            sem = os.at[4 + d]
        else:
            src = pl.ds(span, wbuf.shape[0])
            dst = wbuf.at[:, pl.ds(d * part, part)]
            sem = os.at[d]
        mine = pltpu.make_async_copy(wo.at[src, col], dst, sem)
        other = pltpu.make_async_copy(theirs.at[src, col], dst, sem)
        return mine, other

    def out_start(d, low_rows):
        mine, other = out_load(d, low_rows)

        @pl.when(g == d // 2)
        def _():
            mine.start()

        @pl.when(g != d // 2)
        def _():
            other.start()

    def arrive(r, begin=0, end=3):
        for n in range(begin, end):
            x_arrive(r, coming[n])
            if r < last - 1 and n == 0:
                @pl.when(jnp.logical_not(inner))
                def _():
                    x_own(r + 2)
            if r < last and n == 1:
                @pl.when(inner)
                def _():
                    x_own(r + 1)

    def head_norm(got, gains, dst, to):
        for h in range(span // HD):
            cols = slice(h * HD, (h + 1) * HD)
            vals = got[:, cols]
            scaled = vals * lax.rsqrt(jnp.mean(vals * vals, axis=1, keepdims=True) + 1e-06)
            dst[to, cols] = (scaled * gains[...]).astype(BF)

    def chunk(r):
        lo, size = CUTS[r]
        at = pl.ds(lo, size)
        kept = keep[lo : lo + size]
        sums = jnp.zeros((size, 1), F32)
        squares = jnp.zeros((size, 1), F32)
        for c in range(4):
            vals = xg[c, at, :].astype(F32) * kept
            sums += jnp.sum(vals, axis=1, keepdims=True)
            squares += jnp.sum(vals * vals, axis=1, keepdims=True)
        middle = sums / width
        inv = lax.rsqrt(squares / width - middle * middle + 1e-06)
        for c in range(4):
            cut = slice(c * part, (c + 1) * part)
            vals = xg[c, at, :].astype(F32) * kept
            mod[:size, cut] = (
                (1.0 + md[1, :, cut]) * ((vals - middle) * inv) + md[0, :, cut]
            ).astype(BF)

        def value(i):
            if r == 0:
                wcopy(i).wait()
            at = pl.ds(pl.multiple_of(i * span, span), span)
            return jnp.dot(mod[:size, :], wbuf[:, at], preferred_element_type=F32)

        own = seat(r, me)
        hops = moves(r)
        head_norm(value(1), kg, kbuf, own)
        hops[0].start()
        vbuf[own, :] = value(2).astype(BF)
        hops[1].start()
        head_norm(value(0), qg, q, at)
        if r < last:
            @pl.when(inner)
            def _():
                arrive(r + 1, 0, 2)

        if r == last:
            for trade in trades:
                trade.wait_recv()
            for d in range(3):
                out_start(d, False)

        def tile(i, carry):
            to = pl.ds(pl.multiple_of((i - 3) * span, span), span)
            act[at, to] = jax.nn.gelu(value(i), approximate=True).astype(BF)
            return carry

        if r == last:
            hops[2].start()
            hops[3].start()
        lax.fori_loop(3, tiles, tile, 0)
        if r < last:
            hops[2].start()
            hops[3].start()
        if r == last:
            out_start(3, False)
            for d in range(4):
                out_start(d, True)

    rate = HD ** (-0.5) * 1.4426950408889634

    def attend(begin, end):
        first = begin == 0
        cuts = CUTS[begin:end]
        keys = pl.ds(4 * cuts[0][0], 4 * sum(size for _, size in cuts))
        if first:
            shut[...] = key_mask(tmap, tlen, CUTS, rows)

        def heads(i, carry):
            for j in range(2):
                h = i * 2 + j
                at = pl.ds(pl.multiple_of(h * HD, HD), HD)
                s = lax.dot_general(
                    q[:, at], kbuf[keys, at], (((1,), (1,)), ((), ())), preferred_element_type=F32
                )
                s = s * rate + shut[:, keys]
                top = jnp.max(s, axis=1, keepdims=True)
                if not first:
                    top = jnp.maximum(top, high[h])
                p = jnp.exp2(s - top)
                total = jnp.sum(p, axis=1, keepdims=True)
                got = jnp.dot(p.astype(BF), vbuf[keys, at], preferred_element_type=F32)
                if not first:
                    shrink = jnp.exp2(high[h] - top)
                    total = total + low[h] * shrink
                    got = got + gain[:, at] * shrink
                if end == len(CUTS):
                    att[:, at] = (got / total).astype(BF)
                else:
                    high[h] = top
                    low[h] = total
                    gain[:, at] = got
            return carry

        lax.fori_loop(0, span // (2 * HD), heads, 0)

    arrive(0)
    chunk(0)
    for r in range(1, last + 1):

        @pl.when(inner)
        def _():
            arrive(r, 2, 3)

        kv_relay(r - 1)

        @pl.when(jnp.logical_not(inner))
        def _():
            arrive(r)

        chunk(r)
    kv_relay(last)
    for r in range(last):
        kv_rest(r)
    attend(0, last)
    kv_rest(last)
    attend(last, last + 1)
    for d in range(4):
        for low_rows in (False, True):
            out_load(d, low_rows)[0].wait()

    def hop(r, p, d, way):
        at = pl.ds(r * STEP, STEP)
        slot = d + 1 - way
        return push(
            sbuf.at[p], rbuf.at[slot, at, :], ss.at[p], rs.at[r, slot], "fsdp",
            jnp.clip(z + 1 - 2 * way, 0, 3),
        )

    def share(d, at):
        col = pl.ds(pl.multiple_of(d * part, part), part)
        up = pl.ds(pl.multiple_of((d // 2) * span, span), span)
        side = pl.ds(pl.multiple_of((4 + d % 2) * part, part), part)
        tmp[...] = jnp.dot(
            act[at, :], wbuf[:, col], preferred_element_type=F32
        ) + jnp.dot(att[at, :], wbuf[up, side], preferred_element_type=F32)

    cut = pl.ds(pl.multiple_of(z * part, part), part)
    weighted = head[:, cut].astype(F32) * (1.0 + md[4, :, cut])
    quarter = head.shape[0] // 4
    my_head = head[pl.ds(pl.multiple_of(z * quarter, quarter), quarter), :].astype(F32)
    scale_sum = jnp.sum(my_head * (1.0 + md[4]), axis=1, keepdims=True)
    shift_sum = jnp.sum(my_head * md[3], axis=1, keepdims=True)
    my_image, my_valid = places(tmap, tlen, me * (rows // TILE), (1, rows), 1)
    owner = z // 2

    def order_at(p):
        firsts = pick(z, [3, 3, 0, 0])
        seconds = pick(z, [2, 0, 3, 1])
        thirds = pick(z, [1, 2, 1, 2])
        return jnp.where(p == 0, firsts, jnp.where(p == 1, seconds, thirds))

    def sent_before(r, p):
        d = order_at(p)
        hop(r, p, d, jnp.where(d > z, 0, 1)).wait_send()

    def relays(r):
        at = pl.ds(r * STEP, STEP)

        def relay(p, carry):
            d = order_at(p)
            way = jnp.where(d > z, 0, 1)
            share(d, at)
            if r > 0:
                sent_before(r - 1, p)

            @pl.when(inner)
            def _():
                hop(r, p, d, way).wait_recv()
                tmp[...] += rbuf[d + 1 - way, at, :].astype(F32)

            sbuf[p] = tmp[...].astype(BF)
            hop(r, p, d, way).start()
            return carry

        lax.fori_loop(0, 3, relay, 0)

    def give(r, d, source, at):
        return push(vsend.at[r, d], vrec.at[r, source], us.at[r, at], ur.at[r, source], "fsdp", d)

    def give_up(r):
        at = pl.ds(r * STEP, STEP)
        return pltpu.make_async_copy(upbuf.at[at, :], up_out.at[at, :], uo.at[r])

    def final(r):
        at = pl.ds(r * STEP, STEP)
        share(z, at)

        @pl.when(z > 0)
        def _():
            hop(r, 0, z, 0).wait_recv()
            tmp[...] += rbuf[z + 1, at, :].astype(F32)

        @pl.when(z < 3)
        def _():
            hop(r, 0, z, 1).wait_recv()
            tmp[...] += rbuf[z, at, :].astype(F32)

        kept = keep[r * STEP : (r + 1) * STEP]
        x = hid[at, :].astype(F32) * kept
        up = ((x + md[2, :, cut] * tmp[...]) * kept).astype(BF)
        upbuf[at, :] = up
        give_up(r).start()
        wide = up.astype(F32)
        stats = pack_stats(
            jnp.sum(wide, axis=1, keepdims=True), jnp.sum(wide * wide, axis=1, keepdims=True)
        )
        vpart = lax.dot_general(
            weighted,
            wide,
            (((1,), (1,)), ((), ())),
            precision=lax.Precision.HIGHEST,
            preferred_element_type=F32,
        )
        for d in range(4):
            vsend[r, d, :quarter, :] = vpart[d * quarter : (d + 1) * quarter]
            vsend[r, d, quarter:, :] = stats
        for s in range(1, 4):
            give(r, lax.rem(z + s, 4), z, s - 1).start()

    def vel_move(r, t, source_g, source_z):
        slot = source_g * 2 + lax.rem(source_z, 2)
        return push_to(
            quart.at[r], vel.at[r, slot], vs.at[r, t], vr.at[r, slot],
            {"guide": source_z // 2, "fsdp": lax.rem(z + t, 4)},
        )

    def velocity(r):
        got = vsend[r, z]
        for s in range(1, 4):
            other = lax.rem(z + s, 4)
            give(r, other, other, s - 1).wait_recv()
            got = got + vrec[r, other]
        sums = got[quarter : quarter + 1]
        squares = got[quarter + 1 : quarter + 2]
        middle = sums / width
        inv = lax.rsqrt(squares / width - middle * middle + 1e-06)
        found = inv * (got[:quarter] - middle * scale_sum) + shift_sum
        quart[r] = found
        for t in range(1, 4):
            vel_move(r, t, g, z).start()

        @pl.when(owner != g)
        def _():
            vel_move(r, 0, g, z).start()

        @pl.when(owner == g)
        def _():
            vel[r, g * 2 + lax.rem(z, 2)] = found

        on = slice(r * STEP, (r + 1) * STEP)
        full = jnp.sum(jnp.where(my_valid[:, on], squares, 0.0), axis=1, keepdims=True)
        top = jnp.max(jnp.where(my_image[:, on], found, -jnp.inf), axis=1, keepdims=True)
        return full, jnp.max(top, axis=0, keepdims=True)

    relays(0)
    relays(1)
    final(0)
    relays(2)
    for r in range(last + 1):
        for move in moves(r):
            move.wait_send()
        for c in range(4):
            @pl.when((z < 3) & (z >= c))
            def _():
                x_hop(r, c, 0).wait_send()

            @pl.when((z > 0) & (z <= c))
            def _():
                x_hop(r, c, 1).wait_send()
    for trade in trades:
        trade.wait_send()
    final(1)
    full, top = velocity(0)
    final(2)
    for r in (1, 2):
        more, higher = velocity(r)
        full = full + more
        top = jnp.maximum(top, higher)
    level = lax.broadcasted_iota(jnp.int32, (8, 128), 0)
    tot[z, me] = jnp.where(level == 0, full, top)

    def announce(s, t):
        return push_to(
            tot.at[z, me], tot.at[z, me], ks.at[s, t], kr.at[z, me],
            {"seq": lax.rem(me + s, 4), "fsdp": lax.rem(z + t, 4)},
        )

    pairs = [(s, t) for s in range(4) for t in range(4) if s + t]
    for s, t in pairs:
        announce(s, t).start()
    half = lats.shape[0] // 2
    for r in range(steps):
        for source_g in range(2):
            for turn in range(2):
                slot = source_g * 2 + turn

                @pl.when((g != source_g) | (z != g * 2 + turn))
                def _():
                    push_to(
                        quart.at[r], vel.at[r, slot], vs.at[r, 0], vr.at[r, slot], {"guide": 1 - g}
                    ).wait_recv()

        cond = jnp.concatenate([vel[r, 0], vel[r, 1]], axis=0)
        free = jnp.concatenate([vel[r, 2], vel[r, 3]], axis=0)
        guided = free + guide[...] * (cond - free)
        at = pl.ds(r * STEP, STEP)
        mine = lats[pl.ds(pl.multiple_of(g * half, half), half), at]
        on = slice(r * STEP, (r + 1) * STEP)
        lat_out[:, at] = jnp.where(my_image[:, on], mine + step[...] * guided, 0.0)
    for s, t in pairs:
        there = (lax.rem(z + t, 4), lax.rem(me + s, 4))
        push_to(tot.at[there], tot.at[there], ks.at[s, t], kr.at[there], {"guide": 1 - g}).wait_recv()
    added = tot[z, 0] + tot[z, 1] + tot[z, 2] + tot[z, 3]
    peak = tot[0, 0]
    for s in range(4):
        for t in range(4):
            peak = jnp.maximum(peak, tot[t, s])
    count = (IMG + tlen[...]).astype(F32) * width
    norm_out[...] = jnp.sqrt(added[0:1, 0:1] / count)
    peak_out[...] = peak[1:2, 0:1]
    for r in range(steps):
        give_up(r).wait()
    for p in range(3):
        sent_before(steps - 1, p)
    for r in range(steps):
        for t in range(1, 4):
            give(r, lax.rem(z + t, 4), z, t - 1).wait_send()
            vel_move(r, t, g, z).wait_send()

        @pl.when(owner != g)
        def _():
            vel_move(r, 0, g, z).wait_send()
    for s, t in pairs:
        announce(s, t).wait_send()


def hand_over(up, lat, norm, peak, up_out, lat_out, norm_out, peak_out):
    up_out[...] = up[...]
    lat_out[...] = lat[...]
    norm_out[...] = norm[...]
    peak_out[...] = peak[...]


def vmem(count):
    return [pl.BlockSpec(memory_space=pltpu.VMEM)] * count


def smem(count):
    return [pl.BlockSpec(memory_space=pltpu.SMEM)] * count


def layer(tmap, tlen, guide, step, hid, md, qg, kg, head, lats, w, wo):
    rows, part = hid.shape
    cols = w.shape[1]
    span = (cols - wo.shape[0]) // 2
    wide = cols - 3 * span
    quarter = lats.shape[0] // 4
    chunks = len(CUTS)
    steps = rows // STEP
    dma = pltpu.SemaphoreType.DMA
    shape = jax.ShapeDtypeStruct
    hbm = pl.BlockSpec(memory_space=pltpu.HBM)
    return pl.pallas_call(
        layer_kernel,
        out_shape=(
            shape((rows, part), BF),
            shape((lats.shape[0] // 2, rows), F32),
            shape((1, 1), F32),
            shape((1, 1), F32),
            shape(wo.shape, BF),
        ),
        in_specs=smem(1) + vmem(9) + [hbm, hbm],
        out_specs=(hbm,) + tuple(vmem(3)) + (hbm,),
        scratch_shapes=[
            pltpu.VMEM((4, rows, part), BF),
            pltpu.VMEM(w.shape, BF),
            pltpu.VMEM((max(size for _, size in CUTS), w.shape[0]), BF),
            pltpu.VMEM((rows, span), BF),
        ]
        + [
            pltpu.VMEM((4 * rows, span), BF),
            pltpu.VMEM((4 * rows, span), BF),
            pltpu.VMEM((rows, wide), BF),
            pltpu.VMEM((rows, span), BF),
            pltpu.VMEM((span // HD, rows, 1), F32),
            pltpu.VMEM((span // HD, rows, 1), F32),
            pltpu.VMEM((rows, span), F32),
            pltpu.VMEM((3, STEP, part), BF),
            pltpu.VMEM((5, rows, part), BF),
            pltpu.VMEM((STEP, part), F32),
            pltpu.VMEM((steps, 4, quarter + 8, STEP), F32),
            pltpu.VMEM((steps, 4, quarter + 8, STEP), F32),
            pltpu.VMEM((steps, quarter, STEP), F32),
            pltpu.VMEM((steps, 4, quarter, STEP), F32),
            pltpu.VMEM((4, 4, 8, 128), F32),
            pltpu.VMEM((1, 4 * rows), F32),
            pltpu.VMEM((rows, part), BF),
            dma((7,)),
            dma((2, chunks, 4)),
            dma((chunks, 4)),
            dma((chunks, 6)),
            dma((chunks, 4)),
            dma((chunks, 4)),
            dma((8,)),
            dma((2, 4)),
            dma((3,)),
            dma((steps, 5)),
            dma((steps, 3)),
            dma((steps, 4)),
            dma((steps, 4)),
            dma((steps, 4)),
            dma((4, 4)),
            dma((4, 4)),
            dma((steps,)),
        ],
        compiler_params=pltpu.CompilerParams(
            collective_id=1, has_side_effects=True, vmem_limit_bytes=62 << 20
        ),
        cost_estimate=pl.CostEstimate(
            flops=8 * rows * part * cols, bytes_accessed=8 * part * cols, transcendentals=0
        ),
    )(tmap, tlen, guide, step, hid, md, qg, kg, head, lats, w, wo)


def fast_shards(
    hidden,
    modulation,
    in_weight,
    query_gain,
    key_gain,
    out_weight,
    head_weight,
    latents,
    step_size,
    guidance,
    text_len,
    tile_map,
):
    results = layer(
        tile_map, text_len[None], guidance[None], step_size[None], hidden[0],
        modulation[0, 0][:, None, :], query_gain[None], key_gain[None], head_weight.T, latents,
        in_weight, out_weight,
    )[:4]
    updated, next_latents, norm, peak = pl.pallas_call(
        hand_over,
        out_shape=tuple(jax.ShapeDtypeStruct(x.shape, x.dtype) for x in results),
        in_specs=vmem(4),
        out_specs=tuple(vmem(4)),
    )(*results)
    return (updated[None], next_latents, norm, peak)


def solution(mesh):
    placed = (
        P("guide", "seq", "fsdp"),
        P("guide", None, None, None),
        P(None, "fsdp"),
        P(),
        P(),
        P("fsdp", "guide"),
        P(),
        P(None, "seq"),
        P(),
        P(),
        P(),
        P(),
    )
    shape = dict(mesh.shape)
    planned = shape["fsdp"] == 4 and shape["seq"] == 4 and shape["guide"] == 2

    def chosen(*args):
        return (fast_shards if planned and args[10].shape[0] == 1 else shards)(*args)

    return jax.shard_map(
        chosen,
        mesh=mesh,
        in_specs=placed,
        out_specs=(
            P("guide", "seq", "fsdp"),
            P("guide", "seq"),
            P("guide", None),
            P("guide", None),
        ),
        check_vma=False,
    )
```

```python
import jax
import jax.numpy as jnp
from jax import lax
from jax.experimental import pallas as pl
from jax.experimental.pallas import tpu as pltpu
from jax.sharding import PartitionSpec as P

HD = 128
TXT = 512
IMG = 1024
TILE = 128


def swapped(block, axis, stride):
    count = lax.axis_size(axis)
    route = []
    for low in range(count):
        high = low | 1 << stride
        if high != low and high < count:
            route += [(low, high), (high, low)]
    return lax.ppermute(block, axis, route)


def layer_norm(values):
    middle = jnp.mean(values, axis=-1, keepdims=True)
    power = jnp.mean(values * values, axis=-1, keepdims=True)
    return (values - middle) * lax.rsqrt(power - middle * middle + 1e-06)


def describe(index, tile_map, text_len):
    tile_index = index // TILE
    numbers = jnp.arange(tile_map.shape[0], dtype=jnp.int32)
    picked = jnp.sum(
        jnp.where(tile_index[:, None] == numbers[None, :], tile_map[None, :], 0), axis=1
    )
    logical = picked * TILE + index % TILE
    request = logical // (TXT + IMG)
    position = logical % (TXT + IMG)
    image = position >= TXT
    slots = jnp.arange(text_len.shape[0], dtype=jnp.int32)
    length = jnp.sum(jnp.where(request[:, None] == slots[None, :], text_len[None, :], 0), axis=1)
    valid = image | (position < length)
    return (request, image, valid)


def head_rms(values, gain):
    row_count = values.shape[0]
    shaped = values.reshape(row_count, -1, HD)
    scaled = shaped * lax.rsqrt(jnp.mean(shaped * shaped, axis=-1, keepdims=True) + 1e-06) * gain
    return scaled.reshape(row_count, -1).astype(jnp.bfloat16)


def shards(
    hidden,
    modulation,
    in_weight,
    query_gain,
    key_gain,
    out_weight,
    head_weight,
    latents,
    step_size,
    guidance,
    text_len,
    tile_map,
):
    row_count = hidden.shape[1]
    local_width = hidden.shape[2]
    requests = text_len.shape[0]
    first_row = lax.axis_index("seq") * row_count
    my_request, my_image, my_valid = describe(
        first_row + jnp.arange(row_count, dtype=jnp.int32), tile_map, text_len
    )
    request_hot = (my_request[:, None] == jnp.arange(requests, dtype=jnp.int32)[None, :]).astype(
        jnp.float32
    )

    def lookup(which):
        return jnp.dot(request_hot, modulation[0, :, which, :], precision=lax.Precision.HIGHEST)

    feature_start = lax.axis_index("fsdp") * local_width
    keep = my_valid[:, None]
    x_rows = hidden[0] * keep.astype(jnp.bfloat16)
    whole = lax.all_gather(x_rows, "fsdp", axis=1, tiled=True)
    normed = layer_norm(whole.astype(jnp.float32))
    modded = ((1.0 + lookup(1)) * normed + lookup(0)).astype(jnp.bfloat16)
    col_width = in_weight.shape[1]
    projected = jnp.dot(modded, in_weight, preferred_element_type=jnp.float32)
    span = (col_width - out_weight.shape[0]) // 2
    head_count = span // HD
    queries = head_rms(projected[:, :span], query_gain)
    keys = head_rms(projected[:, span : 2 * span], key_gain)
    values = projected[:, 2 * span : 3 * span].astype(jnp.bfloat16)
    mlp_part = projected[:, 3 * span :]
    query_heads = queries.reshape(row_count, head_count, HD)
    factor = HD ** (-0.5)
    key_piece = lax.all_gather(keys, "seq", axis=0, tiled=True)
    value_piece = lax.all_gather(values, "seq", axis=0, tiled=True)
    width = key_piece.shape[0]
    key_request, key_image, key_valid = describe(
        jnp.arange(width, dtype=jnp.int32), tile_map, text_len
    )
    allowed = (my_request[:, None] == key_request[None, :]) & key_valid[None, :]
    run_max = jnp.full((head_count, row_count), -1e30, jnp.float32)
    key_heads = key_piece.reshape(width, head_count, HD)
    value_heads = value_piece.reshape(width, head_count, HD)
    scores = (
        jnp.einsum("qhd,khd->hqk", query_heads, key_heads, preferred_element_type=jnp.float32)
        * factor
    )
    scores = jnp.where(allowed[None, :, :], scores, -jnp.inf)
    new_max = jnp.maximum(run_max, jnp.max(scores, axis=-1))
    raised = jnp.exp(scores - new_max[:, :, None])
    new_total = jnp.sum(raised, axis=-1)
    added = jnp.einsum(
        "hqk,khd->hqd", raised.astype(jnp.bfloat16), value_heads, preferred_element_type=jnp.float32
    )
    attended = (
        (added / new_total[:, :, None])
        .transpose(1, 0, 2)
        .reshape(row_count, span)
        .astype(jnp.bfloat16)
    )
    activated = jax.nn.gelu(mlp_part, approximate=True).astype(jnp.bfloat16)
    branch = jnp.concatenate([attended, activated], axis=1)
    terms = jnp.dot(
        branch,
        lax.all_gather(out_weight, "guide", axis=1, tiled=True),
        preferred_element_type=jnp.float32,
    )
    mixed = lax.psum_scatter(terms, "fsdp", scatter_dimension=1, tiled=True)
    gate = lax.dynamic_slice_in_dim(lookup(2), feature_start, local_width, 1)
    updated = ((x_rows.astype(jnp.float32) + gate * mixed) * keep.astype(jnp.float32)).astype(
        jnp.bfloat16
    )
    up_values = updated.astype(jnp.float32)
    contract = (((0,), (1,)), ((), ()))
    full_width = local_width * lax.axis_size("fsdp")
    row_sums, row_squares = lax.psum(
        (jnp.sum(up_values, axis=1), jnp.sum(up_values * up_values, axis=1)), "fsdp"
    )
    middle = (row_sums / full_width)[:, None]
    power = (row_squares / full_width)[:, None]
    local_normed = (up_values - middle) * lax.rsqrt(power - middle * middle + 1e-06)
    head_scale = lax.dynamic_slice_in_dim(lookup(4), feature_start, local_width, 1)
    head_shift = lax.dynamic_slice_in_dim(lookup(3), feature_start, local_width, 1)
    final = ((1.0 + head_scale) * local_normed + head_shift).astype(jnp.bfloat16)
    head_rows = lax.dynamic_slice_in_dim(head_weight, feature_start, local_width, 0)
    head_part = lax.dot_general(head_rows, final, contract, preferred_element_type=jnp.float32)
    velocity = lax.psum(head_part, "fsdp")
    partner = swapped(velocity.astype(jnp.bfloat16), "guide", 0).astype(velocity.dtype)
    is_first = lax.axis_index("guide") == 0
    cond_velocity = jnp.where(is_first, velocity, partner)
    uncond_velocity = jnp.where(is_first, partner, velocity)
    guide_rows = jnp.dot(request_hot, guidance, precision=lax.Precision.HIGHEST)
    step_rows = jnp.dot(request_hot, step_size, precision=lax.Precision.HIGHEST)
    guided = uncond_velocity + guide_rows[None, :] * (cond_velocity - uncond_velocity)
    channel_count = latents.shape[0] // lax.axis_size("guide")
    channel_start = lax.axis_index("guide") * channel_count
    my_guided = lax.dynamic_slice_in_dim(guided, channel_start, channel_count, 0)
    my_latents = lax.dynamic_slice_in_dim(latents, channel_start, channel_count, 0)
    next_latents = jnp.where(my_image[None, :], my_latents + step_rows[None, :] * my_guided, 0.0)
    member = my_request[None, :] == jnp.arange(requests, dtype=jnp.int32)[:, None]
    squares = jnp.sum(up_values * up_values, axis=1)
    local_total = jnp.sum(jnp.where(member & my_valid[None, :], squares[None, :], 0.0), axis=1)
    picked = jnp.where((member & my_image[None, :])[:, None, :], velocity[None, :, :], -jnp.inf)
    local_peak = jnp.max(picked, axis=(1, 2))
    total = lax.psum(local_total, ("seq", "fsdp"))
    peak = lax.pmax(local_peak, "seq")
    count = (IMG + text_len).astype(jnp.float32) * (local_width * lax.axis_size("fsdp"))
    hidden_norm = jnp.sqrt(total / count)
    return (updated[None], next_latents, hidden_norm[None], peak[None])


MESH = pl.DeviceIdType.MESH
BF = jnp.bfloat16
F32 = jnp.float32


def greet():
    barrier = pltpu.get_barrier_semaphore()
    g = lax.axis_index("guide")
    me = lax.axis_index("seq")
    z = lax.axis_index("fsdp")
    for s in range(4):
        for t in range(4):
            if s + t:
                ahead = {"seq": lax.rem(me + s, 4), "fsdp": lax.rem(z + t, 4)}
                pl.semaphore_signal(barrier, inc=1, device_id=ahead, device_id_type=MESH)
    for t in range(4):
        ahead = {"guide": 1 - g, "fsdp": lax.rem(z + t, 4)}
        pl.semaphore_signal(barrier, inc=1, device_id=ahead, device_id_type=MESH)
    pl.semaphore_wait(barrier, 19)


def push_to(src, dst, send, recv, target):
    return pltpu.make_async_remote_copy(
        src_ref=src, dst_ref=dst, send_sem=send, recv_sem=recv, device_id=target, device_id_type=MESH
    )


def push(src, dst, send, recv, axis, target):
    return push_to(src, dst, send, recv, {axis: target})


def pack_stats(sums, squares):
    rows = sums.shape[0]
    lane = lax.broadcasted_iota(jnp.int32, (rows, 128), 1)
    both = jnp.where(lane == 0, sums, jnp.where(lane == 1, squares, 0.0))
    return jnp.transpose(both)[:8]


def places(tmap, tlen, first, shape, dim):
    spot = lax.broadcasted_iota(jnp.int32, shape, dim)
    base = jnp.zeros(shape, jnp.int32)
    for j in range(shape[dim] // TILE):
        base = jnp.where(spot >= j * TILE, (tmap[first + j] - j) * TILE, base)
    where = spot + base
    image = where >= TXT
    return image, image | (where < tlen[...])


def row_keep(tmap, tlen, me, rows):
    _, valid = places(tmap, tlen, me * (rows // TILE), (rows, 1), 0)
    return jnp.where(valid, 1.0, 0.0)


def pick(z, values):
    out = values[-1]
    for i in range(len(values) - 2, -1, -1):
        out = jnp.where(z == i, values[i], out)
    return out


CUTS = ((0, 80), (80, 80), (160, 80), (240, 80), (320, 64))
STEP = 128


def key_mask(tmap, tlen, cuts, rows):
    shape = (1, 4 * sum(size for _, size in cuts))
    spot = lax.broadcasted_iota(jnp.int32, shape, 1)
    where = jnp.zeros(shape, jnp.int32)
    here = 0
    for lo, size in cuts:
        for src in range(4):
            row = lo
            while row < lo + size:
                tile = (src * rows + row) // TILE
                base = tmap[tile] * TILE + row % TILE - here
                where = jnp.where(spot >= here, spot + base, where)
                after = min((row // TILE + 1) * TILE, lo + size)
                here += after - row
                row = after
    return jnp.where((where >= TXT) | (where < tlen[...]), 0.0, -1e30)


def layer_kernel(
    tmap, tlen, guide, step, hid, md, qg, kg, head, lats, w, wo,
    up_out, lat_out, norm_out, peak_out, theirs,
    xg, wbuf, mod, q, kbuf, vbuf, act, att, high, low, gain,
    sbuf, rbuf, tmp, vsend, vrec, quart, vel, tot, shut, upbuf,
    ws, xs, xr, ps, kq, vq, os, gw, ss, rs, us, ur, vs, vr, ks, kr, uo,
):
    z = lax.axis_index("fsdp")
    g = lax.axis_index("guide")
    me = lax.axis_index("seq")
    rows, part = hid.shape
    width = part * 4
    span = q.shape[1]
    tiles = w.shape[1] // span
    steps = rows // STEP
    last = len(CUTS) - 1
    inner = (z > 0) & (z < 3)
    near_x = me + 1 - 2 * lax.rem(me, 2)
    near_y = lax.rem(me + 2, 4)
    across = 3 - me

    def wcopy(i):
        at = pl.ds(pl.multiple_of(i * span, span), span)
        return pltpu.make_async_copy(w.at[:, at], wbuf.at[:, at], ws.at[i])

    for i in (1, 2, 0, 3, 4, 5, 6):
        wcopy(i).start()
    greet()

    def x_hop(r, c, way, first=False):
        lo, size = CUTS[r]
        target = jnp.minimum(z + 1, 3) if way == 0 else jnp.maximum(z - 1, 0)
        at = pl.ds(lo, size)
        src = hid.at[at, :] if first else xg.at[c, at, :]
        return push(src, xg.at[c, at, :], xs.at[way, r, c], xr.at[r, c], "fsdp", target)

    def x_own(r):
        @pl.when(z < 3)
        def _():
            x_hop(r, z, 0, True).start()

        @pl.when(z > 0)
        def _():
            x_hop(r, z, 1, True).start()

    def x_arrive(r, c):
        x_hop(r, c, 0).wait_recv()

        @pl.when((c < z) & (z < 3))
        def _():
            x_hop(r, c, 0).start()

        @pl.when((c > z) & (z > 0))
        def _():
            x_hop(r, c, 1).start()

    coming = [
        pick(z, [1, 2, 1, 2]),
        pick(z, [2, 0, 3, 1]),
        pick(z, [3, 3, 0, 0]),
    ]
    x_own(0)

    @pl.when(jnp.logical_not(inner))
    def _():
        x_own(1)

    half_rows = wo.shape[0] // 4
    trades = []
    for i in range(4):
        at = pl.ds(i * half_rows, half_rows)
        trades.append(push(wo.at[at, :], theirs.at[at, :], gw.at[0, i], gw.at[1, i], "guide", 1 - g))
    for trade in trades:
        trade.start()
    keep = row_keep(tmap, tlen, me, rows)
    xg[z] = hid[...]

    def seat(r, src):
        lo, size = CUTS[r]
        return pl.ds(pl.multiple_of(4 * lo + src * size, 16), size)

    def key_hop(r, src, at, target):
        cut = seat(r, src)
        return push(kbuf.at[cut, :], kbuf.at[cut, :], ps.at[r, at], kq.at[r, src], "seq", target)

    def value_hop(r, src, at, target):
        cut = seat(r, src)
        return push(vbuf.at[cut, :], vbuf.at[cut, :], ps.at[r, at], vq.at[r, src], "seq", target)

    def moves(r):
        return [
            key_hop(r, me, 0, near_x),
            value_hop(r, me, 1, near_y),
            key_hop(r, me, 2, near_y),
            value_hop(r, me, 3, near_x),
            key_hop(r, near_x, 4, near_y),
            value_hop(r, near_y, 5, near_x),
        ]

    def kv_relay(r):
        key_hop(r, near_x, 0, near_x).wait_recv()
        moves(r)[4].start()
        value_hop(r, near_y, 1, near_y).wait_recv()
        moves(r)[5].start()

    def kv_rest(r):
        value_hop(r, near_x, 3, near_x).wait_recv()
        key_hop(r, near_y, 2, near_y).wait_recv()
        key_hop(r, across, 4, near_y).wait_recv()
        value_hop(r, across, 5, near_x).wait_recv()

    def out_load(d, low_rows):
        col = pl.ds((d % 2) * part, part)
        if low_rows:
            src = pl.ds(0, span)
            dst = wbuf.at[pl.ds((d // 2) * span, span), pl.ds(4 * part + (d % 2) * part, part)]
            sem = os.at[4 + d]
        else:
            src = pl.ds(span, wbuf.shape[0])
            dst = wbuf.at[:, pl.ds(d * part, part)]
            sem = os.at[d]
        mine = pltpu.make_async_copy(wo.at[src, col], dst, sem)
        other = pltpu.make_async_copy(theirs.at[src, col], dst, sem)
        return mine, other

    def out_start(d, low_rows):
        mine, other = out_load(d, low_rows)

        @pl.when(g == d // 2)
        def _():
            mine.start()

        @pl.when(g != d // 2)
        def _():
            other.start()

    def arrive(r, begin=0, end=3):
        for n in range(begin, end):
            x_arrive(r, coming[n])
            if r < last - 1 and n == 0:
                @pl.when(jnp.logical_not(inner))
                def _():
                    x_own(r + 2)
            if r < last and n == 1:
                @pl.when(inner)
                def _():
                    x_own(r + 1)

    def head_norm(got, gains, dst, to):
        for h in range(span // HD):
            cols = slice(h * HD, (h + 1) * HD)
            vals = got[:, cols]
            scaled = vals * lax.rsqrt(jnp.mean(vals * vals, axis=1, keepdims=True) + 1e-06)
            dst[to, cols] = (scaled * gains[...]).astype(BF)

    def chunk(r):
        lo, size = CUTS[r]
        at = pl.ds(lo, size)
        kept = keep[lo : lo + size]
        sums = jnp.zeros((size, 1), F32)
        squares = jnp.zeros((size, 1), F32)
        for c in range(4):
            vals = xg[c, at, :].astype(F32) * kept
            sums += jnp.sum(vals, axis=1, keepdims=True)
            squares += jnp.sum(vals * vals, axis=1, keepdims=True)
        middle = sums / width
        inv = lax.rsqrt(squares / width - middle * middle + 1e-06)
        for c in range(4):
            cut = slice(c * part, (c + 1) * part)
            vals = xg[c, at, :].astype(F32) * kept
            mod[:size, cut] = (
                (1.0 + md[1, :, cut]) * ((vals - middle) * inv) + md[0, :, cut]
            ).astype(BF)

        def value(i):
            if r == 0:
                wcopy(i).wait()
            at = pl.ds(pl.multiple_of(i * span, span), span)
            return jnp.dot(mod[:size, :], wbuf[:, at], preferred_element_type=F32)

        own = seat(r, me)
        hops = moves(r)
        head_norm(value(1), kg, kbuf, own)
        hops[0].start()
        vbuf[own, :] = value(2).astype(BF)
        hops[1].start()
        head_norm(value(0), qg, q, at)
        if r < last:
            @pl.when(inner)
            def _():
                arrive(r + 1, 0, 2)

        if r == last:
            for trade in trades:
                trade.wait_recv()
            for d in range(3):
                out_start(d, False)

        def tile(i, carry):
            to = pl.ds(pl.multiple_of((i - 3) * span, span), span)
            act[at, to] = jax.nn.gelu(value(i), approximate=True).astype(BF)
            return carry

        if r == last:
            hops[2].start()
            hops[3].start()
        lax.fori_loop(3, tiles, tile, 0)
        if r < last:
            hops[2].start()
            hops[3].start()
        if r == last:
            out_start(3, False)
            for d in range(4):
                out_start(d, True)

    rate = HD ** (-0.5) * 1.4426950408889634

    def attend(begin, end, block):
        first = begin == 0
        on = slice(block * STEP, (block + 1) * STEP)
        cuts = CUTS[begin:end]
        keys = pl.ds(4 * cuts[0][0], 4 * sum(size for _, size in cuts))

        def heads(i, carry):
            for j in range(2):
                h = i * 2 + j
                at = pl.ds(pl.multiple_of(h * HD, HD), HD)
                s = lax.dot_general(
                    q[on, at], kbuf[keys, at], (((1,), (1,)), ((), ())), preferred_element_type=F32
                )
                s = s * rate + shut[:, keys]
                top = jnp.max(s, axis=1, keepdims=True)
                if not first:
                    top = jnp.maximum(top, high[h, on])
                p = jnp.exp2(s - top)
                total = jnp.sum(p, axis=1, keepdims=True)
                got = jnp.dot(p.astype(BF), vbuf[keys, at], preferred_element_type=F32)
                if not first:
                    shrink = jnp.exp2(high[h, on] - top)
                    total = total + low[h, on] * shrink
                    got = got + gain[on, at] * shrink
                if end == len(CUTS):
                    att[on, at] = (got / total).astype(BF)
                else:
                    high[h, on] = top
                    low[h, on] = total
                    gain[on, at] = got
            return carry

        lax.fori_loop(0, span // (2 * HD), heads, 0)

    arrive(0)
    chunk(0)
    for r in range(1, last + 1):

        @pl.when(inner)
        def _():
            arrive(r, 2, 3)

        kv_relay(r - 1)

        @pl.when(jnp.logical_not(inner))
        def _():
            arrive(r)

        chunk(r)
    kv_relay(last)
    for r in range(last):
        kv_rest(r)
    shut[...] = key_mask(tmap, tlen, CUTS, rows)
    for block in range(steps - 1):
        attend(0, last, block)
    kv_rest(last)
    attend(last, last + 1, 0)
    for d in range(4):
        for low_rows in (False, True):
            out_load(d, low_rows)[0].wait()

    def hop(r, p, d, way):
        at = pl.ds(r * STEP, STEP)
        slot = d + 1 - way
        return push(
            sbuf.at[p], rbuf.at[slot, at, :], ss.at[p], rs.at[r, slot], "fsdp",
            jnp.clip(z + 1 - 2 * way, 0, 3),
        )

    def share(d, at):
        col = pl.ds(pl.multiple_of(d * part, part), part)
        up = pl.ds(pl.multiple_of((d // 2) * span, span), span)
        side = pl.ds(pl.multiple_of((4 + d % 2) * part, part), part)
        tmp[...] = jnp.dot(
            act[at, :], wbuf[:, col], preferred_element_type=F32
        ) + jnp.dot(att[at, :], wbuf[up, side], preferred_element_type=F32)

    cut = pl.ds(pl.multiple_of(z * part, part), part)
    weighted = head[:, cut].astype(F32) * (1.0 + md[4, :, cut])
    quarter = head.shape[0] // 4
    my_head = head[pl.ds(pl.multiple_of(z * quarter, quarter), quarter), :].astype(F32)
    scale_sum = jnp.sum(my_head * (1.0 + md[4]), axis=1, keepdims=True)
    shift_sum = jnp.sum(my_head * md[3], axis=1, keepdims=True)
    my_image, my_valid = places(tmap, tlen, me * (rows // TILE), (1, rows), 1)
    owner = z // 2

    def order_at(p):
        firsts = pick(z, [3, 3, 0, 0])
        seconds = pick(z, [2, 0, 3, 1])
        thirds = pick(z, [1, 2, 1, 2])
        return jnp.where(p == 0, firsts, jnp.where(p == 1, seconds, thirds))

    def sent_before(r, p):
        d = order_at(p)
        hop(r, p, d, jnp.where(d > z, 0, 1)).wait_send()

    def relays(r):
        at = pl.ds(r * STEP, STEP)

        def relay(p, carry):
            d = order_at(p)
            way = jnp.where(d > z, 0, 1)
            share(d, at)

            @pl.when(p == 2)
            def _():
                sent_before(r, 0)

            if r > 0:
                @pl.when(p < 2)
                def _():
                    sent_before(r - 1, p + 1)

            @pl.when(inner)
            def _():
                hop(r, p, d, way).wait_recv()
                tmp[...] += rbuf[d + 1 - way, at, :].astype(F32)

            sbuf[p] = tmp[...].astype(BF)
            hop(r, p, d, way).start()
            return carry

        lax.fori_loop(0, 3, relay, 0)

    def give(r, d, source, at):
        return push(vsend.at[r, d], vrec.at[r, source], us.at[r, at], ur.at[r, source], "fsdp", d)

    def give_up(r):
        at = pl.ds(r * STEP, STEP)
        return pltpu.make_async_copy(upbuf.at[at, :], up_out.at[at, :], uo.at[r])

    def final(r):
        at = pl.ds(r * STEP, STEP)
        share(z, at)

        @pl.when(z > 0)
        def _():
            hop(r, 0, z, 0).wait_recv()
            tmp[...] += rbuf[z + 1, at, :].astype(F32)

        @pl.when(z < 3)
        def _():
            hop(r, 0, z, 1).wait_recv()
            tmp[...] += rbuf[z, at, :].astype(F32)

        kept = keep[r * STEP : (r + 1) * STEP]
        x = hid[at, :].astype(F32) * kept
        up = ((x + md[2, :, cut] * tmp[...]) * kept).astype(BF)
        upbuf[at, :] = up
        give_up(r).start()
        wide = up.astype(F32)
        stats = pack_stats(
            jnp.sum(wide, axis=1, keepdims=True), jnp.sum(wide * wide, axis=1, keepdims=True)
        )
        vpart = lax.dot_general(
            weighted,
            wide,
            (((1,), (1,)), ((), ())),
            precision=lax.Precision.HIGHEST,
            preferred_element_type=F32,
        )
        for d in range(4):
            vsend[r, d, :quarter, :] = vpart[d * quarter : (d + 1) * quarter]
            vsend[r, d, quarter:, :] = stats
        for s in range(1, 4):
            give(r, lax.rem(z + s, 4), z, s - 1).start()

    def vel_move(r, t, source_g, source_z):
        slot = source_g * 2 + lax.rem(source_z, 2)
        return push_to(
            quart.at[r], vel.at[r, slot], vs.at[r, t], vr.at[r, slot],
            {"guide": source_z // 2, "fsdp": lax.rem(z + t, 4)},
        )

    def velocity(r):
        got = vsend[r, z]
        for s in range(1, 4):
            other = lax.rem(z + s, 4)
            give(r, other, other, s - 1).wait_recv()
            got = got + vrec[r, other]
        sums = got[quarter : quarter + 1]
        squares = got[quarter + 1 : quarter + 2]
        middle = sums / width
        inv = lax.rsqrt(squares / width - middle * middle + 1e-06)
        found = inv * (got[:quarter] - middle * scale_sum) + shift_sum
        quart[r] = found
        for t in range(1, 4):
            vel_move(r, t, g, z).start()

        @pl.when(owner != g)
        def _():
            vel_move(r, 0, g, z).start()

        @pl.when(owner == g)
        def _():
            vel[r, g * 2 + lax.rem(z, 2)] = found

        on = slice(r * STEP, (r + 1) * STEP)
        full = jnp.sum(jnp.where(my_valid[:, on], squares, 0.0), axis=1, keepdims=True)
        top = jnp.max(jnp.where(my_image[:, on], found, -jnp.inf), axis=1, keepdims=True)
        return full, jnp.max(top, axis=0, keepdims=True)

    relays(0)
    attend(last, last + 1, 1)
    relays(1)
    attend(0, last, 2)
    attend(last, last + 1, 2)
    final(0)
    relays(2)
    for r in range(last + 1):
        for move in moves(r):
            move.wait_send()
        for c in range(4):
            @pl.when((z < 3) & (z >= c))
            def _():
                x_hop(r, c, 0).wait_send()

            @pl.when((z > 0) & (z <= c))
            def _():
                x_hop(r, c, 1).wait_send()
    for trade in trades:
        trade.wait_send()
    final(1)
    full, top = velocity(0)
    final(2)
    for r in (1, 2):
        more, higher = velocity(r)
        full = full + more
        top = jnp.maximum(top, higher)
    level = lax.broadcasted_iota(jnp.int32, (8, 128), 0)
    tot[z, me] = jnp.where(level == 0, full, top)

    def announce(s, t):
        return push_to(
            tot.at[z, me], tot.at[z, me], ks.at[s, t], kr.at[z, me],
            {"seq": lax.rem(me + s, 4), "fsdp": lax.rem(z + t, 4)},
        )

    pairs = [(s, t) for s in range(4) for t in range(4) if s + t]
    for s, t in pairs:
        announce(s, t).start()
    half = lats.shape[0] // 2
    for r in range(steps):
        for source_g in range(2):
            for turn in range(2):
                slot = source_g * 2 + turn

                @pl.when((g != source_g) | (z != g * 2 + turn))
                def _():
                    push_to(
                        quart.at[r], vel.at[r, slot], vs.at[r, 0], vr.at[r, slot], {"guide": 1 - g}
                    ).wait_recv()

        cond = jnp.concatenate([vel[r, 0], vel[r, 1]], axis=0)
        free = jnp.concatenate([vel[r, 2], vel[r, 3]], axis=0)
        guided = free + guide[...] * (cond - free)
        at = pl.ds(r * STEP, STEP)
        mine = lats[pl.ds(pl.multiple_of(g * half, half), half), at]
        on = slice(r * STEP, (r + 1) * STEP)
        lat_out[:, at] = jnp.where(my_image[:, on], mine + step[...] * guided, 0.0)
    for s, t in pairs:
        there = (lax.rem(z + t, 4), lax.rem(me + s, 4))
        push_to(tot.at[there], tot.at[there], ks.at[s, t], kr.at[there], {"guide": 1 - g}).wait_recv()
    added = tot[z, 0] + tot[z, 1] + tot[z, 2] + tot[z, 3]
    peak = tot[0, 0]
    for s in range(4):
        for t in range(4):
            peak = jnp.maximum(peak, tot[t, s])
    count = (IMG + tlen[...]).astype(F32) * width
    norm_out[...] = jnp.sqrt(added[0:1, 0:1] / count)
    peak_out[...] = peak[1:2, 0:1]
    for r in range(steps):
        give_up(r).wait()
    for p in (1, 2):
        sent_before(steps - 1, p)
    for r in range(steps):
        for t in range(1, 4):
            give(r, lax.rem(z + t, 4), z, t - 1).wait_send()
            vel_move(r, t, g, z).wait_send()

        @pl.when(owner != g)
        def _():
            vel_move(r, 0, g, z).wait_send()
    for s, t in pairs:
        announce(s, t).wait_send()


def hand_over(up, lat, norm, peak, up_out, lat_out, norm_out, peak_out):
    up_out[...] = up[...]
    lat_out[...] = lat[...]
    norm_out[...] = norm[...]
    peak_out[...] = peak[...]


def vmem(count):
    return [pl.BlockSpec(memory_space=pltpu.VMEM)] * count


def smem(count):
    return [pl.BlockSpec(memory_space=pltpu.SMEM)] * count


def layer(tmap, tlen, guide, step, hid, md, qg, kg, head, lats, w, wo):
    rows, part = hid.shape
    cols = w.shape[1]
    span = (cols - wo.shape[0]) // 2
    wide = cols - 3 * span
    quarter = lats.shape[0] // 4
    chunks = len(CUTS)
    steps = rows // STEP
    dma = pltpu.SemaphoreType.DMA
    shape = jax.ShapeDtypeStruct
    hbm = pl.BlockSpec(memory_space=pltpu.HBM)
    return pl.pallas_call(
        layer_kernel,
        out_shape=(
            shape((rows, part), BF),
            shape((lats.shape[0] // 2, rows), F32),
            shape((1, 1), F32),
            shape((1, 1), F32),
            shape(wo.shape, BF),
        ),
        in_specs=smem(1) + vmem(9) + [hbm, hbm],
        out_specs=(hbm,) + tuple(vmem(3)) + (hbm,),
        scratch_shapes=[
            pltpu.VMEM((4, rows, part), BF),
            pltpu.VMEM(w.shape, BF),
            pltpu.VMEM((max(size for _, size in CUTS), w.shape[0]), BF),
            pltpu.VMEM((rows, span), BF),
        ]
        + [
            pltpu.VMEM((4 * rows, span), BF),
            pltpu.VMEM((4 * rows, span), BF),
            pltpu.VMEM((rows, wide), BF),
            pltpu.VMEM((rows, span), BF),
            pltpu.VMEM((span // HD, rows, 1), F32),
            pltpu.VMEM((span // HD, rows, 1), F32),
            pltpu.VMEM((rows, span), F32),
            pltpu.VMEM((3, STEP, part), BF),
            pltpu.VMEM((5, rows, part), BF),
            pltpu.VMEM((STEP, part), F32),
            pltpu.VMEM((steps, 4, quarter + 8, STEP), F32),
            pltpu.VMEM((steps, 4, quarter + 8, STEP), F32),
            pltpu.VMEM((steps, quarter, STEP), F32),
            pltpu.VMEM((steps, 4, quarter, STEP), F32),
            pltpu.VMEM((4, 4, 8, 128), F32),
            pltpu.VMEM((1, 4 * rows), F32),
            pltpu.VMEM((rows, part), BF),
            dma((7,)),
            dma((2, chunks, 4)),
            dma((chunks, 4)),
            dma((chunks, 6)),
            dma((chunks, 4)),
            dma((chunks, 4)),
            dma((8,)),
            dma((2, 4)),
            dma((3,)),
            dma((steps, 5)),
            dma((steps, 3)),
            dma((steps, 4)),
            dma((steps, 4)),
            dma((steps, 4)),
            dma((4, 4)),
            dma((4, 4)),
            dma((steps,)),
        ],
        compiler_params=pltpu.CompilerParams(
            collective_id=1, has_side_effects=True, vmem_limit_bytes=62 << 20
        ),
        cost_estimate=pl.CostEstimate(
            flops=8 * rows * part * cols, bytes_accessed=8 * part * cols, transcendentals=0
        ),
    )(tmap, tlen, guide, step, hid, md, qg, kg, head, lats, w, wo)


def fast_shards(
    hidden,
    modulation,
    in_weight,
    query_gain,
    key_gain,
    out_weight,
    head_weight,
    latents,
    step_size,
    guidance,
    text_len,
    tile_map,
):
    results = layer(
        tile_map, text_len[None], guidance[None], step_size[None], hidden[0],
        modulation[0, 0][:, None, :], query_gain[None], key_gain[None], head_weight.T, latents,
        in_weight, out_weight,
    )[:4]
    updated, next_latents, norm, peak = pl.pallas_call(
        hand_over,
        out_shape=tuple(jax.ShapeDtypeStruct(x.shape, x.dtype) for x in results),
        in_specs=vmem(4),
        out_specs=tuple(vmem(4)),
    )(*results)
    return (updated[None], next_latents, norm, peak)


def solution(mesh):
    placed = (
        P("guide", "seq", "fsdp"),
        P("guide", None, None, None),
        P(None, "fsdp"),
        P(),
        P(),
        P("fsdp", "guide"),
        P(),
        P(None, "seq"),
        P(),
        P(),
        P(),
        P(),
    )
    shape = dict(mesh.shape)
    planned = shape["fsdp"] == 4 and shape["seq"] == 4 and shape["guide"] == 2

    def chosen(*args):
        return (fast_shards if planned and args[10].shape[0] == 1 else shards)(*args)

    return jax.shard_map(
        chosen,
        mesh=mesh,
        in_specs=placed,
        out_specs=(
            P("guide", "seq", "fsdp"),
            P("guide", "seq"),
            P("guide", None),
            P("guide", None),
        ),
        check_vma=False,
    )
```
